32 devices in a mesh: region: 2 (over x), grid: 16 (over z, y, core).
Axes of the slice: x: 2, y: 2, z: 4, core: 2. Of those that a mesh axis runs over, the one named last changes fastest.
Arguments:
- radar_subimages: bfloat16 [768, 4, 2, 128, 128], P(('region', 'grid')), parts along dimension 0, may hold values from -25 to 25, as said below
- owning_sector: int32 [768, 1], P(('region', 'grid')), parts along dimension 0, may hold values from 0 to 15; in each aligned block of 24 rows (0 to 23, 24 to 47, ...) at most 2 rows name the same one
- sector_down_start: int32 [768], P(('region', 'grid')), parts along dimension 0, may hold values from 0 to 3
- sector_across_start: int32 [768], P(('region', 'grid')), parts along dimension 0, may hold values from 0 to 7
Outputs:
- coherence: float32 [3, 4096, 256], P(None, ('region', 'grid')), parts along dimension 1
The draws below stay inside these ranges and needn't reach their ends.
There are 2 independent parts, one for each index of `region`. The reference program is written for one: setup_inputs(seed, part) draws one part's arguments, and reference() takes and returns one part's arrays. A program takes and returns all parts, laid end to end along the dimension named above; each array names one. Nothing has to cross between parts.
Inputs may be any that keep to these rules, and one draw needn't show every extreme that they name: `owning_sector`: the blocks of one device name any one tile at most 2 times, and some device's blocks name a tile exactly 2 times. `radar_subimages`: speckled complex samples whose dates are partly correlated with one another.
All inputs are finite; a program needn't handle non-finite values.
Results may differ from the reference program's by a relative error of at most 0.0003.
Values may be sent and summed in bfloat16 or wider, within the bound.
No kernel may reach another device: no remote copies, remote signals or barrier semaphores. Data moves between devices by JAX's collectives and lax.ppermute only.
A program may use at most 128 MiB of HBM per device.

```python
import math
import jax
import jax.numpy as jnp
import numpy as np

CELL_PIXEL_SPAN = 128
VISIT_TIMES = 4
SUBIMAGE_BOUND = 2
SUBIMAGES_HELD = 24
TILE_TALL_PARTS = 4
TILE_WIDE_PARTS = 8
CELL_TOTAL_SUM = 384
SLOTS = 32
N_GRID = 16


def draw_radar_subimages(key, part):
    first, second, tertiary_term, quadruple_product = jax.random.split(key, 4)
    lattice_extent = (CELL_TOTAL_SUM, 1, 2, CELL_PIXEL_SPAN, CELL_PIXEL_SPAN)
    product_dimension = (CELL_TOTAL_SUM, VISIT_TIMES, 2, CELL_PIXEL_SPAN, CELL_PIXEL_SPAN)
    common = jnp.clip(jax.random.normal(first, lattice_extent, jnp.float32), -4.0, 4.0)
    noise = jnp.clip(jax.random.normal(second, product_dimension, jnp.float32), -4.0, 4.0)
    echo_magnitude = jnp.exp(jax.random.uniform(tertiary_term, (CELL_TOTAL_SUM, 1, 1, CELL_PIXEL_SPAN, CELL_PIXEL_SPAN), jnp.float32, math.log(0.3), math.log(3.0)))
    mean_fraction = jax.random.uniform(quadruple_product, (CELL_TOTAL_SUM, VISIT_TIMES, 1, 1, 1), jnp.float32, 0.1, 0.95)
    mixed = mean_fraction * common + jnp.sqrt(1.0 - mean_fraction * mean_fraction) * noise
    return (echo_magnitude * mixed).astype(jnp.bfloat16)


def set_ends(array, stream_key, smallest, high):
    extent = array.shape
    index_at = [jax.random.randint(jax.random.fold_in(stream_key, axis), (), 0, extent[axis]) for axis in range(len(extent))]
    array = array.at[tuple(index_at)].set(smallest)
    longest = extent.index(max(extent))
    index_at[longest] = (index_at[longest] + 1) % extent[longest]
    return array.at[tuple(index_at)].set(high)


def shared_out(key, own, number, rows, number_of, top, limit, skew):
    order = jax.random.permutation(key, number_of)
    packed, ordinary = load_shares(number_of, rows * top, limit, skew, True), load_shares(number_of, rows * top, limit, skew, False)
    places = jnp.arange(number_of)

    def named(sizes, rotation):
        used = int((sizes > 0).sum())
        fixed = max(1, used // 4)
        shifted = fixed + (places - fixed + rotation * (used - fixed)) % max(1, number_of - fixed)
        return jnp.zeros((number_of,), jnp.int32).at[order[jnp.where(places < fixed, places, shifted)]].set(jnp.asarray(sizes, jnp.int32))

    sizes = jnp.where(number % 4 == 0, named(packed, number // 4), named(ordinary, number - number // 4 - 1))
    mixed = jax.random.permutation(jax.random.fold_in(own, 3), number_of)
    donor, receiver = mixed[0:number_of // 2 * 2:2], mixed[1:number_of // 2 * 2:2]
    slack = jnp.minimum(sizes[donor] - 1, limit - sizes[receiver]) // 2
    slack = jnp.where((donor == order[0]) | (receiver == order[0]) | (sizes[receiver] == 0), 0, jnp.maximum(slack, 0))
    shifted = jax.random.randint(jax.random.fold_in(own, 4), (number_of // 2,), 0, 1 << 20) % (slack + 1)
    sizes = sizes.at[donor].add(-shifted).at[receiver].add(shifted)
    labels = jnp.searchsorted(jnp.cumsum(sizes), jnp.arange(rows * top), side="right").astype(jnp.int32)
    grid = labels.reshape(top, rows).T
    grid = grid[jax.random.permutation(jax.random.fold_in(own, 1), rows)]
    rotation = jax.random.randint(jax.random.fold_in(own, 2), (rows, 1), 0, top)
    return jnp.take_along_axis(grid, (jnp.arange(top)[None, :] + rotation) % top, axis=1)


def load_shares(amount, total, bound, skew, full):
    loads = [(1 << 20) // math.isqrt(standing ** skew) + 1 for standing in range(1, amount + 1)]
    largest = bound if full else min(bound, max(-(-total // amount), total * loads[0] // sum(loads)))
    least = 1 if total - largest >= amount - 1 else 0
    given, rest = [largest] + [least] * (amount - 1), total - largest - least * (amount - 1)
    while rest > 0:
        free = [i for i in range(1, amount) if given[i] < largest] or [i for i in range(1, amount) if given[i] < bound]
        whole, budget = sum([loads[i] for i in free]), rest
        for i in free:
            addition = min(bound - given[i], max(1, budget * loads[i] // whole), rest)
            given[i] = given[i] + addition
            rest = rest - addition
    return np.array(given)


def setup_inputs(seed: int = 0, part: int = 0) -> dict:
    key_list = jax.random.split(jax.random.key(seed), 5)
    part_keys = jax.random.split(jax.random.fold_in(key_list[4], part), 5)
    radar_subimages = draw_radar_subimages(jax.random.fold_in(jax.random.fold_in(key_list[4], part), 71), part)
    owning_sector_keys = jax.random.split(jax.random.fold_in(part_keys[1], 1), CELL_TOTAL_SUM // SUBIMAGES_HELD)
    owning_sector_turns = jax.random.permutation(jax.random.fold_in(part_keys[1], 3), CELL_TOTAL_SUM // SUBIMAGES_HELD)
    owning_sector = jax.vmap(lambda own, number: shared_out(jax.random.fold_in(part_keys[1], 2), own, number, SUBIMAGES_HELD, N_GRID, 1, SUBIMAGE_BOUND, 2))(owning_sector_keys, owning_sector_turns).reshape((CELL_TOTAL_SUM, 1))
    sector_down_start = set_ends(jax.random.randint(part_keys[2], (CELL_TOTAL_SUM,), 0, TILE_TALL_PARTS), jax.random.fold_in(part_keys[2], 1), 0, TILE_TALL_PARTS - 1).astype(jnp.int32)
    sector_across_start = set_ends(jax.random.randint(part_keys[3], (CELL_TOTAL_SUM,), 0, TILE_WIDE_PARTS), jax.random.fold_in(part_keys[3], 1), 0, TILE_WIDE_PARTS - 1).astype(jnp.int32)
    return {"radar_subimages": radar_subimages, "owning_sector": owning_sector, "sector_down_start": sector_down_start, "sector_across_start": sector_across_start}


EPSILON = 1e-06

def box_sum(fields):
    row_total = fields.shape[1]
    col_total = fields.shape[2]
    row_out = row_total // 4
    col_out = col_total // 4
    padded = jnp.pad(fields, ((0, 0), (2, 2), (12, 12)))
    col_sums = sum((padded[:, :, shift_index:shift_index + 4 * col_out:4] for shift_index in range(28)))
    row_sums = sum((col_sums[:, 1 + shift_index:1 + shift_index + 4 * row_out:4, :] for shift_index in range(7)))
    return row_sums

def reference(radar_subimages, owning_sector, sector_down_start, sector_across_start):
    sector_entry_label = owning_sector[:, 0] * SLOTS + sector_down_start * TILE_WIDE_PARTS + sector_across_start
    entry_capacity = N_GRID * SLOTS
    sector_entry_accrual = jax.ops.segment_sum(radar_subimages.astype(jnp.float32), sector_entry_label, num_segments=entry_capacity)
    counts = jax.ops.segment_sum(jnp.ones_like(sector_entry_label), sector_entry_label, num_segments=entry_capacity)
    merged_image = sector_entry_accrual / jnp.maximum(counts, 1).astype(jnp.float32)[:, None, None, None, None]
    merged_image = merged_image.reshape(N_GRID, TILE_TALL_PARTS, TILE_WIDE_PARTS, VISIT_TIMES, 2, CELL_PIXEL_SPAN, CELL_PIXEL_SPAN)
    merged_image = merged_image.transpose(3, 4, 0, 1, 5, 2, 6).reshape(VISIT_TIMES, 2, N_GRID * TILE_TALL_PARTS * CELL_PIXEL_SPAN, TILE_WIDE_PARTS * CELL_PIXEL_SPAN)
    real_part = merged_image[:, 0]
    imag_part = merged_image[:, 1]
    cross_re = real_part[:-1] * real_part[1:] + imag_part[:-1] * imag_part[1:]
    cross_im = imag_part[:-1] * real_part[1:] - real_part[:-1] * imag_part[1:]
    powers = real_part * real_part + imag_part * imag_part
    fields = jnp.concatenate([cross_re, cross_im, powers], 0)
    box_sums = box_sum(fields)
    couple_tally_value = VISIT_TIMES - 1
    magnitude = jnp.sqrt(box_sums[:couple_tally_value] ** 2 + box_sums[couple_tally_value:2 * couple_tally_value] ** 2)
    scale_root = jnp.sqrt(box_sums[2 * couple_tally_value:3 * couple_tally_value] * box_sums[2 * couple_tally_value + 1:] + EPSILON)
    return magnitude / scale_root
```

```python
import functools

import jax
import jax.numpy as jnp
from jax import lax
from jax.experimental import pallas as pl
from jax.experimental.pallas import tpu as pltpu
from jax.sharding import PartitionSpec as P

TILE_TALL_PARTS = 4
TILE_WIDE_PARTS = 8
EPSILON = 1e-06
LANES = 128


def cut_kernel(me_ref, cells_ref, *refs, date, rows):
    outs, sem = refs[:-1], refs[-1]
    me = me_ref[0]
    copies = []
    for m, out in enumerate(outs):
        start = pl.multiple_of((me ^ m) * rows, rows)
        copies.append(pltpu.make_async_copy(cells_ref.at[:, date, :, pl.ds(start, rows), :], out, sem.at[m]))
    for copy in copies:
        copy.start()
    for copy in copies:
        copy.wait()


def cut(me, cells, date, group):
    held, _, _, side, _ = cells.shape
    rows = side // group
    piece = jax.ShapeDtypeStruct((held, 2, rows, side), cells.dtype)
    return pl.pallas_call(
        functools.partial(cut_kernel, date=date, rows=rows),
        out_shape=[piece] * group,
        grid_spec=pltpu.PrefetchScalarGridSpec(
            num_scalar_prefetch=1,
            grid=(),
            in_specs=[pl.BlockSpec(memory_space=pl.ANY)],
            out_specs=[pl.BlockSpec(memory_space=pl.ANY)] * group,
            scratch_shapes=[pltpu.SemaphoreType.DMA((group,))],
        ),
        name=f"cut_{date}",
    )(me, cells)


def date_kernel(me_ref, slot_ref, share_ref, *refs, group, first, last):
    pieces, refs = refs[:group], refs[group:]
    window_ref, refs = refs[0], refs[1:]
    if first:
        before_ref = None
    else:
        before_ref, refs = refs[0], refs[1:]
    if last:
        (own_ref, up_ref, down_ref), refs = refs[:3], refs[3:]
        comp_ref, refs = refs[0], refs[1:]
    else:
        (comp_ref, own_ref, up_ref, down_ref), refs = refs[:4], refs[4:]
    sums_ref = refs[0]
    if not first:
        old_ref, sem = refs[1:]
        fetch = pltpu.make_async_copy(before_ref, old_ref, sem)
        fetch.start()
    wide, _, lines, rows, side = comp_ref.shape
    held = pieces[0].shape[0]
    me = me_ref[0]
    comp_ref[...] = jnp.zeros(comp_ref.shape, jnp.float32)
    for m, piece in enumerate(pieces):
        base = (me ^ m) * held

        def add(k, carry, piece=piece, base=base):
            slot = slot_ref[base + k]
            share = share_ref[base + k]
            line, across = slot // wide, slot % wide
            for q in range(2):
                comp_ref[across, q, line] += piece[k, q].astype(jnp.float32) * share
            return carry

        lax.fori_loop(0, held, add, 0, unroll=4)
    if not first:
        fetch.wait()
    step = min(lines, 16)
    window = window_ref[...]

    def row_of(ref, q, at):
        return jnp.concatenate(
            [ref[c, q, pl.ds(at, step)].reshape(step * rows, side) for c in range(wide)], axis=1
        )

    def emit(index, field, at):
        high = field.astype(jnp.bfloat16)
        low = (field - high.astype(jnp.float32)).astype(jnp.bfloat16)
        total = jnp.dot(high, window, preferred_element_type=jnp.float32)
        total += jnp.dot(low, window, preferred_element_type=jnp.float32)
        for half in range(sums_ref.shape[1]):
            sums_ref[index, half, pl.ds(at * rows, step * rows), :] = total[:, half * LANES : (half + 1) * LANES]

    for number in range(lines // step):
        at = number * step
        re, im = row_of(comp_ref, 0, at), row_of(comp_ref, 1, at)
        emit(0, re * re + im * im, at)
        if not first:
            re_old, im_old = row_of(old_ref, 0, at), row_of(old_ref, 1, at)
            emit(1, re_old * re + im_old * im, at)
            emit(2, im_old * re - re_old * im, at)
    for f in range(sums_ref.shape[0]):
        lanes = [
            jnp.concatenate(
                [sums_ref[f, half, pl.ds(y, lines, stride=rows), :] for half in range(sums_ref.shape[1])], axis=1
            )
            for y in range(rows)
        ]
        for i in range(rows // 4):
            own_ref[f, i] = sum(lanes[max(0, 4 * i - 1) : min(rows, 4 * i + 6)][1:], lanes[max(0, 4 * i - 1)])
        up = lanes[0] + lanes[1]
        down = lanes[rows - 1]
        index = lax.broadcasted_iota(jnp.int32, up.shape, 0)
        up_next = jnp.where(index == lines - 1, 0.0, pltpu.roll(up, lines - 1, 0))
        down_next = jnp.where(index == 0, 0.0, pltpu.roll(down, 1, 0))
        up_ref[f] = jnp.where(me == 0, up_next, up)
        down_ref[f] = jnp.where(me == group - 1, down_next, down)


def date_step(me, slots, shares, pieces, window, before, last):
    group = len(pieces)
    held, _, rows, side = pieces[0].shape
    lines = group * TILE_TALL_PARTS
    out_cols = window.shape[1]
    first = before is None
    fields = 1 if first else 3
    comp = jax.ShapeDtypeStruct((TILE_WIDE_PARTS, 2, lines, rows, side), jnp.float32)
    outs = [
        jax.ShapeDtypeStruct((fields, rows // 4, lines, out_cols), jnp.float32),
        jax.ShapeDtypeStruct((fields, lines, out_cols), jnp.float32),
        jax.ShapeDtypeStruct((fields, lines, out_cols), jnp.float32),
    ]
    if not last:
        outs = [comp] + outs
    vmem = pl.BlockSpec(memory_space=pltpu.VMEM)
    scratch = [pltpu.VMEM((fields, out_cols // LANES, lines * rows, LANES), jnp.float32)]
    if last:
        scratch = [pltpu.VMEM(comp.shape, comp.dtype)] + scratch
    if not first:
        scratch += [pltpu.VMEM(comp.shape, comp.dtype), pltpu.SemaphoreType.DMA(())]
    result = pl.pallas_call(
        functools.partial(date_kernel, group=group, first=first, last=last),
        out_shape=outs,
        grid_spec=pltpu.PrefetchScalarGridSpec(
            num_scalar_prefetch=3,
            grid=(),
            in_specs=[vmem] * (group + 1) + ([] if first else [pl.BlockSpec(memory_space=pl.ANY)]),
            out_specs=[vmem] * len(outs),
            scratch_shapes=scratch,
        ),
        name="date_step",
    )(me, slots, shares, *pieces, window, *([] if first else [before]))
    return (None, *result) if last else tuple(result)


def local(radar_subimages, owning_sector, sector_down_start, sector_across_start):
    group = lax.axis_size("grid")
    held, dates, _, side, _ = radar_subimages.shape
    cols = TILE_WIDE_PARTS * side
    index = lax.axis_index("grid")
    me = index[None].astype(jnp.int32)
    slot = (
        owning_sector[:, 0] * (TILE_TALL_PARTS * TILE_WIDE_PARTS)
        + sector_down_start * TILE_WIDE_PARTS
        + sector_across_start
    )
    slots = lax.all_to_all(
        jnp.broadcast_to(slot[None], (group, held)), "grid", split_axis=0, concat_axis=0, tiled=True
    ).reshape(group * held)
    counts = jnp.sum((slots[:, None] == slots[None, :]).astype(jnp.int32), axis=1)
    shares = 1.0 / jnp.maximum(counts, 1).astype(jnp.float32)
    col = jnp.arange(cols)[:, None]
    out_col = jnp.arange(cols // 4)[None, :]
    window = ((col >= 4 * out_col - 12) & (col <= 4 * out_col + 15)).astype(jnp.bfloat16)

    comp = None
    sums = []
    for date in range(dates):
        sends = cut(me, radar_subimages, date, group)
        pieces = [sends[0]] + [
            lax.ppermute(sends[m], "grid", [(i, i ^ m) for i in range(group)]) for m in range(1, group)
        ]
        comp, own, up, down = date_step(me, slots, shares, pieces, window, comp, date == dates - 1)
        below = lax.ppermute(up, "grid", [(i, (i - 1) % group) for i in range(group)])
        above = lax.ppermute(down, "grid", [(i, (i + 1) % group) for i in range(group)])
        own = own.at[:, 0].add(above)
        own = own.at[:, -1].add(below)
        sums.append(own)
    results = []
    for k in range(dates - 1):
        magnitude = jnp.sqrt(sums[k + 1][1] ** 2 + sums[k + 1][2] ** 2)
        results.append(magnitude / jnp.sqrt(sums[k][0] * sums[k + 1][0] + EPSILON))
    ready = jnp.stack(results)
    ready = ready.reshape(dates - 1, -1, group, TILE_TALL_PARTS, cols // 4).transpose(2, 0, 1, 3, 4)
    mine = lax.all_to_all(ready, "grid", split_axis=0, concat_axis=0, tiled=True)
    return mine.transpose(1, 3, 0, 2, 4).reshape(dates - 1, TILE_TALL_PARTS * side // 4, cols // 4)


def solution(mesh):
    in_specs = (
        P(("region", "grid"), None, None, None, None),
        P(("region", "grid"), None),
        P(("region", "grid")),
        P(("region", "grid")),
    )
    out_specs = P(None, ("region", "grid"), None)
    return jax.shard_map(local, mesh=mesh, in_specs=in_specs, out_specs=out_specs, check_vma=False)
```

```python
import functools

import jax
import jax.numpy as jnp
from jax import lax
from jax.experimental import pallas as pl
from jax.experimental.pallas import tpu as pltpu
from jax.sharding import PartitionSpec as P


TILE_TALL_PARTS = 4
TILE_WIDE_PARTS = 8
EPSILON = 1e-06
LANES = 128
CHUNKS = (2, 1, 1)


def spans(dates):
    out = []
    for size in CHUNKS:
        out.append((sum(s for _, s in out), size))
    if sum(CHUNKS) != dates:
        out = [(d, 1) for d in range(dates)]
    return out


def strip_of(device, group):
    if group % 4:
        return device
    column, side, core = device // 4, (device // 2) % 2, device % 2
    return side * (group // 2) + 2 * (column + side * (group // 4 - 1 - 2 * column)) + core


def device_at(group):
    places = [strip_of(d, group) for d in range(group)]
    return [places.index(s) for s in range(group)]


def cut_kernel(strip_ref, cells_ref, *refs, tagged):
    tag_ref, outs = (refs[0], refs[1:]) if tagged else (None, refs)
    for m, out in enumerate(outs):
        held, span, planes, _, rows, side = cells_ref.shape
        count = held * span * planes
        out[:count] = cells_ref[:, :, :, strip_ref[m]].reshape(count, rows, side)
        if tagged:
            out[count] = tag_ref[...]


def cut(strips, cells, tag, begin, span):
    held, _, planes, group, rows, side = cells.shape
    tagged = tag is not None
    piece = (held * span * planes + tagged, rows, side)
    cells_spec = pl.BlockSpec(
        (held, pl.Element(span), planes, group, rows, side), lambda i, strips: (0, begin, 0, 0, 0, 0)
    )
    if begin % span == 0:
        cells_spec = pl.BlockSpec(
            (held, span, planes, group, rows, side), lambda i, strips: (0, begin // span, 0, 0, 0, 0)
        )
    return pl.pallas_call(
        functools.partial(cut_kernel, tagged=tagged),
        out_shape=[jax.ShapeDtypeStruct(piece, cells.dtype)] * group,
        grid_spec=pltpu.PrefetchScalarGridSpec(
            num_scalar_prefetch=1,
            grid=(1,),
            in_specs=[cells_spec] + [pl.BlockSpec((rows, side), lambda i, strips: (0, 0))] * tagged,
            out_specs=[pl.BlockSpec(piece, lambda i, strips: (0, 0, 0))] * group,
        ),
        name="cut",
    )(strips, cells, *([tag] if tagged else []))


def step_kernel(strip_ref, place_ref, share_ref, *refs, group, held, span, first, last):
    pieces, window_ref, refs = refs[:group], refs[group], refs[group + 1 :]
    if not first:
        before_ref, refs = refs[0], refs[1:]
    kept = [] if last else [refs[0]]
    refs = refs if last else refs[1:]
    own_ref, up_ref, down_ref, sums_ref = refs[:4]
    refs = refs[4:]
    fresh = span if last else span - 1
    comps = list(refs[:fresh]) + kept
    if not first:
        old_ref, sem = refs[fresh:]
        fetch = pltpu.make_async_copy(before_ref, old_ref, sem)
        fetch.start()
    slots, planes, rows, side = comps[0].shape
    wide = window_ref.shape[0] // side
    lines = slots // wide
    strip = strip_ref[0]
    for comp in comps:
        comp[...] = jnp.zeros(comp.shape, jnp.float32)
    for m, piece in enumerate(pieces):

        def add(k, carry, m=m, piece=piece):
            place = place_ref[m * held + k]
            share = share_ref[m * held + k]
            for d, comp in enumerate(comps):
                for q in range(planes):
                    comp[place, q] += piece[(k * span + d) * planes + q].astype(jnp.float32) * share
            return carry

        lax.fori_loop(0, held, add, 0, unroll=4)
    if not first:
        fetch.wait()
        comps = [old_ref] + comps
    step = min(lines, 16)
    window = window_ref[...]

    def row_of(comp, q, at):
        parts = [comp[pl.ds(c * lines + at, step), q].reshape(step * rows, side) for c in range(wide)]
        return jnp.concatenate(parts, axis=1)

    def emit(index, field, at):
        high = field.astype(jnp.bfloat16)
        low = (field - high.astype(jnp.float32)).astype(jnp.bfloat16)
        total = jnp.dot(high, window, preferred_element_type=jnp.float32)
        total += jnp.dot(low, window, preferred_element_type=jnp.float32)
        for half in range(sums_ref.shape[1]):
            sums_ref[index, half, pl.ds(at * rows, step * rows), :] = total[:, half * LANES : (half + 1) * LANES]

    for number in range(lines // step):
        at = number * step
        index = 0
        re_old = im_old = None
        for d, comp in enumerate(comps):
            re, im = row_of(comp, 0, at), row_of(comp, 1, at)
            if first or d:
                emit(index, re * re + im * im, at)
                index += 1
            if d:
                emit(index, re_old * re + im_old * im, at)
                emit(index + 1, im_old * re - re_old * im, at)
                index += 2
            re_old, im_old = re, im
    for f in range(sums_ref.shape[0]):
        level = [
            jnp.concatenate(
                [sums_ref[f, half, pl.ds(y, lines, stride=rows), :] for half in range(sums_ref.shape[1])], axis=1
            )
            for y in range(rows)
        ]
        for i in range(rows // 4):
            begin, end = max(0, 4 * i - 1), min(rows, 4 * i + 6)
            own_ref[f, i] = sum(level[begin + 1 : end], level[begin])
        up, down = level[0] + level[1], level[rows - 1]
        line = lax.broadcasted_iota(jnp.int32, up.shape, 0)
        up_next = jnp.where(line == lines - 1, 0.0, pltpu.roll(up, lines - 1, 0))
        down_next = jnp.where(line == 0, 0.0, pltpu.roll(down, 1, 0))
        up_ref[f] = jnp.where(strip == 0, up_next, up)
        down_ref[f] = jnp.where(strip == group - 1, down_next, down)


def chunk_step(strips, places, shares, pieces, window, before, span, last):
    group = len(pieces)
    held = places.shape[0] // group
    _, rows, side = pieces[0].shape
    lines = group * TILE_TALL_PARTS
    out_cols = window.shape[1]
    first = before is None
    fields = 3 * span - 2 * first
    comp = jax.ShapeDtypeStruct((lines * TILE_WIDE_PARTS, 2, rows, side), jnp.float32)
    outs = [] if last else [comp]
    outs += [
        jax.ShapeDtypeStruct((fields, rows // 4, lines, out_cols), jnp.float32),
        jax.ShapeDtypeStruct((fields, lines, out_cols), jnp.float32),
        jax.ShapeDtypeStruct((fields, lines, out_cols), jnp.float32),
    ]
    scratch = [pltpu.VMEM((fields, out_cols // LANES, lines * rows, LANES), jnp.float32)]
    scratch += [pltpu.VMEM(comp.shape, comp.dtype)] * (span if last else span - 1)
    if not first:
        scratch += [pltpu.VMEM(comp.shape, comp.dtype), pltpu.SemaphoreType.DMA(())]
    vmem = pl.BlockSpec(memory_space=pltpu.VMEM)
    result = pl.pallas_call(
        functools.partial(step_kernel, group=group, held=held, span=span, first=first, last=last),
        out_shape=outs,
        grid_spec=pltpu.PrefetchScalarGridSpec(
            num_scalar_prefetch=3,
            grid=(),
            in_specs=[vmem] * (group + 1) + ([] if first else [pl.BlockSpec(memory_space=pl.ANY)]),
            out_specs=[vmem] * len(outs),
            scratch_shapes=scratch,
        ),
        name="chunk_step",
    )(strips, places, shares, *pieces, window, *([] if first else [before]))
    return (None, *result) if last else tuple(result)


def local(radar_subimages, owning_sector, sector_down_start, sector_across_start):
    group = lax.axis_size("grid")
    held, dates, planes, side, _ = radar_subimages.shape
    rows = side // group
    lines = group * TILE_TALL_PARTS
    cols = TILE_WIDE_PARTS * side
    me = lax.axis_index("grid").astype(jnp.int32)
    strips = strip_of(me ^ jnp.arange(group, dtype=jnp.int32), group)
    at = device_at(group)
    line = owning_sector[:, 0] * TILE_TALL_PARTS + sector_down_start
    tag = jnp.zeros((rows, side), radar_subimages.dtype)
    tag = tag.at[0, :held].set(line.astype(tag.dtype)).at[1, :held].set(sector_across_start.astype(tag.dtype))
    col = jnp.arange(cols)[:, None]
    out_col = jnp.arange(cols // 4)[None, :]
    window = ((col >= 4 * out_col - 12) & (col <= 4 * out_col + 15)).astype(jnp.bfloat16)

    cells = radar_subimages.reshape(held, dates, planes, group, rows, side)
    chunks = spans(dates)
    order = sorted(range(1, group), reverse=True)
    arrived = []
    for number, (begin, span) in enumerate(chunks):
        sends = cut(strips, cells, None if number else tag, begin, span)
        pieces = [sends[0]] + [None] * (group - 1)
        for m in order:
            pieces[m] = lax.ppermute(sends[m], "grid", [(i, i ^ m) for i in range(group)])
        arrived.append(pieces)

    tags = jnp.stack([piece[-1, :2, :held] for piece in arrived[0]]).astype(jnp.int32)
    places = (tags[:, 1] * lines + tags[:, 0]).reshape(group * held)
    counts = jnp.sum((places[:, None] == places[None, :]).astype(jnp.int32), axis=1)
    shares = 1.0 / jnp.maximum(counts, 1).astype(jnp.float32)

    comp = None
    power, cross = [], []
    for number, (begin, span) in enumerate(chunks):
        comp, own, up, down = chunk_step(
            strips, places, shares, arrived[number], window, comp, span, number == len(chunks) - 1
        )
        below = lax.ppermute(up, "grid", [(at[s], at[s - 1]) for s in range(group)])
        above = lax.ppermute(down, "grid", [(at[s - 1], at[s]) for s in range(group)])
        own = own.at[:, 0].add(above)
        own = own.at[:, -1].add(below)
        index = 0
        for d in range(begin, begin + span):
            power.append(own[index])
            index += 1
            if d:
                cross.append((own[index], own[index + 1]))
                index += 2
    ready = jnp.stack(
        [
            jnp.sqrt(re**2 + im**2) / jnp.sqrt(power[k] * power[k + 1] + EPSILON)
            for k, (re, im) in enumerate(cross)
        ]
    )
    ready = ready.reshape(dates - 1, -1, group, TILE_TALL_PARTS, cols // 4).transpose(2, 0, 1, 3, 4)
    mine = lax.all_to_all(ready, "grid", split_axis=0, concat_axis=0, tiled=True)
    if group % 4 == 0:
        mine = mine.reshape(group // 4, 2, 2, *mine.shape[1:])
        mine = jnp.concatenate([mine[:, 0], mine[::-1, 1]]).reshape(group, *mine.shape[3:])
    return mine.transpose(1, 3, 0, 2, 4).reshape(dates - 1, TILE_TALL_PARTS * side // 4, cols // 4)


def solution(mesh):
    in_specs = (
        P(("region", "grid"), None, None, None, None),
        P(("region", "grid"), None),
        P(("region", "grid")),
        P(("region", "grid")),
    )
    out_specs = P(None, ("region", "grid"), None)

    return jax.shard_map(local, mesh=mesh, in_specs=in_specs, out_specs=out_specs, check_vma=False)
```

```python
import functools

import jax
import jax.numpy as jnp
from jax import lax
from jax.experimental import pallas as pl
from jax.experimental.pallas import tpu as pltpu
from jax.sharding import PartitionSpec as P


TILE_TALL_PARTS = 4
TILE_WIDE_PARTS = 8
EPSILON = 1e-06
LANES = 128
CHUNKS = (2, 1, 1)


def spans(dates):
    out = []
    for size in CHUNKS:
        out.append((sum(s for _, s in out), size))
    if sum(CHUNKS) != dates:
        out = [(d, 1) for d in range(dates)]
    return out


def strip_of(device, group):
    if group % 4:
        return device
    column, side, core = device // 4, (device // 2) % 2, device % 2
    return side * (group // 2) + 2 * (column + side * (group // 4 - 1 - 2 * column)) + core


def device_at(group):
    places = [strip_of(d, group) for d in range(group)]
    return [places.index(s) for s in range(group)]


def cut_kernel(strip_ref, cells_ref, *refs, tagged):
    held, span, planes, group, rows, side = cells_ref.shape
    count = held * span * planes
    if tagged:
        tag_ref, out = refs
        outs = [out.at[m] for m in range(group)]
    else:
        outs = refs
    for m, out in enumerate(outs):
        out[:count] = cells_ref[:, :, :, strip_ref[m]].reshape(count, rows, side)
        if tagged:
            out[count] = tag_ref[...]


def cut(strips, cells, tag, begin, span):
    held, _, planes, group, rows, side = cells.shape
    tagged = tag is not None
    piece = (held * span * planes + tagged, rows, side)
    cells_spec = pl.BlockSpec(
        (held, pl.Element(span), planes, group, rows, side), lambda i, strips: (0, begin, 0, 0, 0, 0)
    )
    if begin % span == 0:
        cells_spec = pl.BlockSpec(
            (held, span, planes, group, rows, side), lambda i, strips: (0, begin // span, 0, 0, 0, 0)
        )
    if tagged:
        pieces, specs = [(group, *piece)], [pl.BlockSpec((group, *piece), lambda i, strips: (0, 0, 0, 0))]
    else:
        pieces, specs = [piece] * group, [pl.BlockSpec(piece, lambda i, strips: (0, 0, 0))] * group
    return pl.pallas_call(
        functools.partial(cut_kernel, tagged=tagged),
        out_shape=[jax.ShapeDtypeStruct(p, cells.dtype) for p in pieces],
        grid_spec=pltpu.PrefetchScalarGridSpec(
            num_scalar_prefetch=1,
            grid=(1,),
            in_specs=[cells_spec] + [pl.BlockSpec((rows, side), lambda i, strips: (0, 0))] * tagged,
            out_specs=specs,
        ),
        name="cut",
    )(strips, cells, *([tag] if tagged else []))


def step_kernel(strip_ref, place_ref, share_ref, *refs, group, held, span, first, last):
    if first:
        pieces, window_ref, refs = [refs[0].at[m] for m in range(group)], refs[1], refs[2:]
    else:
        pieces, window_ref, refs = refs[:group], refs[group], refs[group + 1 :]
    if not first:
        before_ref, refs = refs[0], refs[1:]
    kept = [] if last else [refs[0]]
    refs = refs if last else refs[1:]
    own_ref, up_ref, down_ref, sums_ref = refs[:4]
    refs = refs[4:]
    fresh = span if last else span - 1
    comps = list(refs[:fresh]) + kept
    if not first:
        old_ref, sem = refs[fresh:]
        fetch = pltpu.make_async_copy(before_ref, old_ref, sem)
        fetch.start()
    slots, planes, rows, side = comps[0].shape
    wide = window_ref.shape[0] // side
    lines = slots // wide
    strip = strip_ref[0]
    for comp in comps:
        comp[...] = jnp.zeros(comp.shape, jnp.float32)
    for m, piece in enumerate(pieces):

        def add(k, carry, m=m, piece=piece):
            place = place_ref[m * held + k]
            share = share_ref[m * held + k]
            for d, comp in enumerate(comps):
                for q in range(planes):
                    comp[place, q] += piece[(k * span + d) * planes + q].astype(jnp.float32) * share
            return carry

        lax.fori_loop(0, held, add, 0, unroll=4)
    if not first:
        fetch.wait()
        comps = [old_ref] + comps
    step = min(lines, 16)
    window = window_ref[...]

    def row_of(comp, q, at):
        parts = [comp[pl.ds(c * lines + at, step), q].reshape(step * rows, side) for c in range(wide)]
        return jnp.concatenate(parts, axis=1)

    def emit(index, field, at):
        high = field.astype(jnp.bfloat16)
        low = (field - high.astype(jnp.float32)).astype(jnp.bfloat16)
        total = jnp.dot(high, window, preferred_element_type=jnp.float32)
        total += jnp.dot(low, window, preferred_element_type=jnp.float32)
        for half in range(sums_ref.shape[1]):
            sums_ref[index, half, pl.ds(at * rows, step * rows), :] = total[:, half * LANES : (half + 1) * LANES]

    for number in range(lines // step):
        at = number * step
        index = 0
        re_old = im_old = None
        for d, comp in enumerate(comps):
            re, im = row_of(comp, 0, at), row_of(comp, 1, at)
            if first or d:
                emit(index, re * re + im * im, at)
                index += 1
            if d:
                emit(index, re_old * re + im_old * im, at)
                emit(index + 1, im_old * re - re_old * im, at)
                index += 2
            re_old, im_old = re, im
    for f in range(sums_ref.shape[0]):
        level = [
            jnp.concatenate(
                [sums_ref[f, half, pl.ds(y, lines, stride=rows), :] for half in range(sums_ref.shape[1])], axis=1
            )
            for y in range(rows)
        ]
        for i in range(rows // 4):
            begin, end = max(0, 4 * i - 1), min(rows, 4 * i + 6)
            own_ref[f, i] = sum(level[begin + 1 : end], level[begin])
        up, down = level[0] + level[1], level[rows - 1]
        line = lax.broadcasted_iota(jnp.int32, up.shape, 0)
        up_next = jnp.where(line == lines - 1, 0.0, pltpu.roll(up, lines - 1, 0))
        down_next = jnp.where(line == 0, 0.0, pltpu.roll(down, 1, 0))
        up_ref[f] = jnp.where(strip == 0, up_next, up)
        down_ref[f] = jnp.where(strip == group - 1, down_next, down)


def chunk_step(strips, places, shares, pieces, window, before, span, last):
    group, held = strips.shape[0], places.shape[0] // strips.shape[0]
    rows, side = pieces[0].shape[-2:]
    lines = group * TILE_TALL_PARTS
    out_cols = window.shape[1]
    first = before is None
    fields = 3 * span - 2 * first
    comp = jax.ShapeDtypeStruct((lines * TILE_WIDE_PARTS, 2, rows, side), jnp.float32)
    outs = [] if last else [comp]
    outs += [
        jax.ShapeDtypeStruct((fields, rows // 4, lines, out_cols), jnp.float32),
        jax.ShapeDtypeStruct((fields, lines, out_cols), jnp.float32),
        jax.ShapeDtypeStruct((fields, lines, out_cols), jnp.float32),
    ]
    scratch = [pltpu.VMEM((fields, out_cols // LANES, lines * rows, LANES), jnp.float32)]
    scratch += [pltpu.VMEM(comp.shape, comp.dtype)] * (span if last else span - 1)
    if not first:
        scratch += [pltpu.VMEM(comp.shape, comp.dtype), pltpu.SemaphoreType.DMA(())]
    vmem = pl.BlockSpec(memory_space=pltpu.VMEM)
    result = pl.pallas_call(
        functools.partial(step_kernel, group=group, held=held, span=span, first=first, last=last),
        out_shape=outs,
        grid_spec=pltpu.PrefetchScalarGridSpec(
            num_scalar_prefetch=3,
            grid=(),
            in_specs=[vmem] * (len(pieces) + 1) + ([] if first else [pl.BlockSpec(memory_space=pl.ANY)]),
            out_specs=[vmem] * len(outs),
            scratch_shapes=scratch,
        ),
        name="chunk_step",
    )(strips, places, shares, *pieces, window, *([] if first else [before]))
    return (None, *result) if last else tuple(result)


def local(radar_subimages, owning_sector, sector_down_start, sector_across_start):
    group = lax.axis_size("grid")
    held, dates, planes, side, _ = radar_subimages.shape
    rows = side // group
    lines = group * TILE_TALL_PARTS
    cols = TILE_WIDE_PARTS * side
    me = lax.axis_index("grid").astype(jnp.int32)
    devices = jnp.arange(group, dtype=jnp.int32)
    strips = strip_of(me ^ devices, group)
    at = device_at(group)
    line = owning_sector[:, 0] * TILE_TALL_PARTS + sector_down_start
    tag = jnp.zeros((rows, side), radar_subimages.dtype)
    tag = tag.at[0, :held].set(line.astype(tag.dtype)).at[1, :held].set(sector_across_start.astype(tag.dtype))
    col = jnp.arange(cols)[:, None]
    out_col = jnp.arange(cols // 4)[None, :]
    window = ((col >= 4 * out_col - 12) & (col <= 4 * out_col + 15)).astype(jnp.bfloat16)

    cells = radar_subimages.reshape(held, dates, planes, group, rows, side)
    chunks = spans(dates)
    order = sorted(range(1, group), reverse=True)
    arrived = []
    for number, (begin, span) in enumerate(chunks):
        if number == 0:
            (sends,) = cut(strip_of(devices, group), cells, tag, begin, span)
            arrived.append([lax.all_to_all(sends, "grid", split_axis=0, concat_axis=0, tiled=True)])
            continue
        sends = cut(strips, cells, None, begin, span)
        pieces = [sends[0]] + [None] * (group - 1)
        for m in order:
            pieces[m] = lax.ppermute(sends[m], "grid", [(i, i ^ m) for i in range(group)])
        arrived.append(pieces)

    tags = arrived[0][0][:, -1, :2, :held].astype(jnp.int32)
    places = tags[:, 1] * lines + tags[:, 0]
    places = places.reshape(group * held)
    counts = jnp.sum((places[:, None] == places[None, :]).astype(jnp.int32), axis=1)
    shares = 1.0 / jnp.maximum(counts, 1).astype(jnp.float32)
    tables = [(places, shares), tuple(t.reshape(group, held)[me ^ devices].reshape(group * held) for t in (places, shares))]

    comp = None
    power, cross = [], []
    for number, (begin, span) in enumerate(chunks):
        comp, own, up, down = chunk_step(
            strips, *tables[number > 0], arrived[number], window, comp, span, number == len(chunks) - 1
        )
        below = lax.ppermute(up, "grid", [(at[s], at[s - 1]) for s in range(group)])
        above = lax.ppermute(down, "grid", [(at[s - 1], at[s]) for s in range(group)])
        own = own.at[:, 0].add(above)
        own = own.at[:, -1].add(below)
        index = 0
        for d in range(begin, begin + span):
            power.append(own[index])
            index += 1
            if d:
                cross.append((own[index], own[index + 1]))
                index += 2
    ready = jnp.stack(
        [
            jnp.sqrt(re**2 + im**2) / jnp.sqrt(power[k] * power[k + 1] + EPSILON)
            for k, (re, im) in enumerate(cross)
        ]
    )
    ready = ready.reshape(dates - 1, -1, group, TILE_TALL_PARTS, cols // 4).transpose(2, 0, 1, 3, 4)
    mine = lax.all_to_all(ready, "grid", split_axis=0, concat_axis=0, tiled=True)
    if group % 4 == 0:
        mine = mine.reshape(group // 4, 2, 2, *mine.shape[1:])
        mine = jnp.concatenate([mine[:, 0], mine[::-1, 1]]).reshape(group, *mine.shape[3:])
    return mine.transpose(1, 3, 0, 2, 4).reshape(dates - 1, TILE_TALL_PARTS * side // 4, cols // 4)


def solution(mesh):
    in_specs = (
        P(("region", "grid"), None, None, None, None),
        P(("region", "grid"), None),
        P(("region", "grid")),
        P(("region", "grid")),
    )
    out_specs = P(None, ("region", "grid"), None)

    return jax.shard_map(local, mesh=mesh, in_specs=in_specs, out_specs=out_specs, check_vma=False)
```

```python
import functools

import jax
import jax.numpy as jnp
from jax import lax
from jax.experimental import pallas as pl
from jax.experimental.pallas import tpu as pltpu
from jax.sharding import PartitionSpec as P


TALL = 4
WIDE = 8
EPSILON = 1e-06
LATE = False
LANES = 128
VMEM = pl.BlockSpec(memory_space=pltpu.VMEM)
HBM = pl.BlockSpec(memory_space=pltpu.HBM)


def strip_of(device, group):
    if group % 4:
        return device
    column, side, core = device // 4, (device // 2) % 2, device % 2
    return side * (group // 2) + 2 * (column + side * (group // 4 - 1 - 2 * column)) + core


def device_at(group):
    places = [strip_of(d, group) for d in range(group)]
    return [places.index(s) for s in range(group)]


def bulk_kernel(*refs, span):
    words, (cells_ref, out_ref, *bufs, in_buf, out_buf, tag_buf, word_sem, in_sem, out_sem) = refs[:3], refs[3:]
    parts, each = in_buf.shape[:2]
    group, _, rows, side = out_buf.shape
    planes = in_buf.shape[3]
    held = parts * each
    many = each * span * planes
    fetches = [
        pltpu.make_async_copy(cells_ref.at[pl.ds(j * each, each), pl.ds(0, span)], in_buf.at[j], in_sem.at[j])
        for j in range(parts)
    ]
    small = [pltpu.make_async_copy(word, buf, word_sem.at[n]) for n, (word, buf) in enumerate(zip(words, bufs))]
    for fetch in small + fetches:
        fetch.start()
    for fetch in small:
        fetch.wait()
    owner_ref, down_ref, across_ref = bufs
    tag_buf[...] = jnp.zeros(tag_buf.shape, jnp.float32)
    tag_buf[0:1, :held] = (owner_ref[...] * TALL + down_ref[...]).astype(jnp.float32)
    tag_buf[1:2, :held] = across_ref[...].astype(jnp.float32)
    tag = tag_buf[...].astype(out_buf.dtype)
    stores = []
    for j, fetch in enumerate(fetches):
        fetch.wait()
        more = j == parts - 1
        for g in range(group):
            strip = strip_of(g, group)
            out_buf[g, j * many : (j + 1) * many] = in_buf[j, :, :, :, strip].reshape(many, rows, side)
            if more:
                out_buf[g, held * span * planes] = tag
            piece = pl.ds(j * many, many + more)
            stores.append(pltpu.make_async_copy(out_buf.at[g, piece], out_ref.at[g, piece], out_sem.at[j, g]))
            stores[-1].start()
    for store in stores:
        store.wait()


def bulk_cut(owner, down, across, cells, span):
    held, _, planes, group, rows, side = cells.shape
    parts = next(p for p in (4, 3, 2, 1) if held % p == 0)
    out = jax.ShapeDtypeStruct((group, held * span * planes + 1, rows, side), cells.dtype)
    return pl.pallas_call(
        functools.partial(bulk_kernel, span=span),
        out_shape=pltpu.HBM(out.shape, out.dtype),
        in_specs=[HBM] * 4,
        out_specs=HBM,
        scratch_shapes=[
            *[pltpu.VMEM((1, held), jnp.int32)] * 3,
            pltpu.VMEM((parts, held // parts, span, planes, group, rows, side), cells.dtype),
            pltpu.VMEM(out.shape, out.dtype),
            pltpu.VMEM((rows, side), jnp.float32),
            pltpu.SemaphoreType.DMA((3,)),
            pltpu.SemaphoreType.DMA((parts,)),
            pltpu.SemaphoreType.DMA((parts, group)),
        ],
        compiler_params=pltpu.CompilerParams(vmem_limit_bytes=24 << 20),
        name="bulk_cut",
    )(owner, down, across, cells)


def cut_kernel(strip_ref, cells_ref, *outs):
    held, _, planes, _, rows, side = cells_ref.shape
    for m, out in enumerate(outs):
        out[...] = cells_ref[:, 0, :, strip_ref[m]].reshape(held * planes, rows, side)


def cut(strips, cells, date):
    held, _, planes, group, rows, side = cells.shape
    piece = (held * planes, rows, side)
    return pl.pallas_call(
        cut_kernel,
        out_shape=[jax.ShapeDtypeStruct(piece, cells.dtype)] * group,
        grid_spec=pltpu.PrefetchScalarGridSpec(
            num_scalar_prefetch=1,
            grid=(1,),
            in_specs=[pl.BlockSpec((held, 1, planes, group, rows, side), lambda i, strips: (0, date, 0, 0, 0, 0))],
            out_specs=[pl.BlockSpec(piece, lambda i, strips: (0, 0, 0))] * group,
        ),
        compiler_params=pltpu.CompilerParams(vmem_limit_bytes=16 << 20),
        name="cut",
    )(strips, cells)


def gather(place_ref, share_ref, pieces, comps, base, held):
    span, planes = len(comps), comps[0].shape[1]
    for m, piece in enumerate(pieces):

        def add(k, carry, m=m, piece=piece):
            place = place_ref[(base + m) * held + k]
            share = share_ref[(base + m) * held + k]
            for d, comp in enumerate(comps):
                for q in range(planes):
                    comp[place, q] += piece[(k * span + d) * planes + q].astype(jnp.float32) * share
            return carry

        lax.fori_loop(0, held, add, 0, unroll=4)


def box_sums(strip, comps, window_ref, sums_ref, own_ref, up_ref, down_ref, group, skip):
    slots, _, rows, side = comps[0].shape
    lines = slots // WIDE
    step = min(lines, 16)
    window = window_ref[...]

    def row_of(comp, q, at):
        parts = [comp[pl.ds(c * lines + at, step), q].reshape(step * rows, side) for c in range(WIDE)]
        return jnp.concatenate(parts, axis=1)

    def emit(index, field, at):
        high = field.astype(jnp.bfloat16)
        low = (field - high.astype(jnp.float32)).astype(jnp.bfloat16)
        total = jnp.dot(high, window, preferred_element_type=jnp.float32)
        total += jnp.dot(low, window, preferred_element_type=jnp.float32)
        for half in range(sums_ref.shape[1]):
            sums_ref[index, half, pl.ds(at * rows, step * rows), :] = total[:, half * LANES : (half + 1) * LANES]

    for number in range(lines // step):
        at = number * step
        index = 0
        re_old = im_old = None
        for d, comp in enumerate(comps):
            re, im = row_of(comp, 0, at), row_of(comp, 1, at)
            if d >= skip:
                emit(index, re * re + im * im, at)
                index += 1
            if d:
                emit(index, re_old * re + im_old * im, at)
                emit(index + 1, im_old * re - re_old * im, at)
                index += 2
            re_old, im_old = re, im
    for f in range(sums_ref.shape[0]):
        level = [
            jnp.concatenate(
                [sums_ref[f, half, pl.ds(y, lines, stride=rows), :] for half in range(sums_ref.shape[1])], axis=1
            )
            for y in range(rows)
        ]
        for i in range(rows // 4):
            begin, end = max(0, 4 * i - 1), min(rows, 4 * i + 6)
            own_ref[f, i] = sum(level[begin + 1 : end], level[begin])
        up, down = level[0] + level[1], level[rows - 1]
        line = lax.broadcasted_iota(jnp.int32, up.shape, 0)
        up_next = jnp.where(line == lines - 1, 0.0, pltpu.roll(up, lines - 1, 0))
        down_next = jnp.where(line == 0, 0.0, pltpu.roll(down, 1, 0))
        up_ref[f] = jnp.where(strip == 0, up_next, up)
        down_ref[f] = jnp.where(strip == group - 1, down_next, down)


def bulk_step_kernel(strip_ref, place_ref, share_ref, got_ref, window_ref, kept_ref, own_ref, up_ref, down_ref, sums_ref, *fresh, group, held):
    comps = [*fresh, kept_ref]
    for comp in comps:
        comp[...] = jnp.zeros(comp.shape, jnp.float32)
    gather(place_ref, share_ref, [got_ref.at[m] for m in range(group)], comps, 0, held)
    box_sums(strip_ref[0], comps, window_ref, sums_ref, own_ref, up_ref, down_ref, group, 0)


def step_kernel(strip_ref, place_ref, share_ref, *refs, group, held):
    pieces, (window_ref, before_ref, comp, own_ref, up_ref, down_ref, sums_ref) = refs[:-7], refs[-7:]
    comp[...] = jnp.zeros(comp.shape, jnp.float32)
    gather(place_ref, share_ref, pieces, [comp], 0, held)
    box_sums(strip_ref[0], [before_ref, comp], window_ref, sums_ref, own_ref, up_ref, down_ref, group, 1)


def part_kernel(place_ref, share_ref, *refs, base, held):
    pieces, comp = refs[:-1], refs[-1]
    comp[...] = jnp.zeros(comp.shape, jnp.float32)
    gather(place_ref, share_ref, pieces, [comp], base, held)


def last_step_kernel(strip_ref, place_ref, share_ref, *refs, group, base, held):
    pieces, (window_ref, before_ref, part_ref, comp, own_ref, up_ref, down_ref, sums_ref) = refs[:-8], refs[-8:]
    del part_ref
    gather(place_ref, share_ref, pieces, [comp], base, held)
    box_sums(strip_ref[0], [before_ref, comp], window_ref, sums_ref, own_ref, up_ref, down_ref, group, 1)


def sums_of(fields, rows, lines, cols):
    outs = [(fields, rows // 4, lines, cols), (fields, lines, cols), (fields, lines, cols)]
    return [jax.ShapeDtypeStruct(s, jnp.float32) for s in outs], pltpu.VMEM((fields, cols // LANES, lines * rows, LANES), jnp.float32)


def call(kernel, prefetch, args, outs, scratch=(), aliases=None, mib=16):
    return pl.pallas_call(
        kernel,
        out_shape=outs,
        grid_spec=pltpu.PrefetchScalarGridSpec(
            num_scalar_prefetch=len(prefetch),
            grid=(),
            in_specs=[VMEM] * len(args),
            out_specs=[VMEM] * len(outs),
            scratch_shapes=list(scratch),
        ),
        input_output_aliases=aliases or {},
        compiler_params=pltpu.CompilerParams(vmem_limit_bytes=mib << 20),
    )(*prefetch, *args)


def whole_sum(own_ref, above_ref, below_ref, f, i):
    total = own_ref[f, i]
    if i == 0:
        total = total + above_ref[f]
    if i == own_ref.shape[1] - 1:
        total = total + below_ref[f]
    return total


def coherence(re, im, first, second):
    return jnp.sqrt(re * re + im * im) / jnp.sqrt(first * second + EPSILON)


def deal(out_ref, at, value):
    for g in range(out_ref.shape[0]):
        out_ref[g, at : at + TALL] = value[g * TALL : (g + 1) * TALL]


def bulk_finish_kernel(own_ref, above_ref, below_ref, next_ref, next_above_ref, next_below_ref, out_ref, power_ref, *, span):
    tall = own_ref.shape[1]
    for i in range(tall):
        powers = []
        for d in range(span):
            at = 0 if d == 0 else 3 * d - 2
            powers.append(whole_sum(own_ref, above_ref, below_ref, at, i))
            if d:
                re, im = (whole_sum(own_ref, above_ref, below_ref, at + n, i) for n in (1, 2))
                deal(out_ref, ((d - 1) * tall + i) * TALL, coherence(re, im, powers[-2], powers[-1]))
        power, re, im = (whole_sum(next_ref, next_above_ref, next_below_ref, n, i) for n in range(3))
        deal(out_ref, ((span - 1) * tall + i) * TALL, coherence(re, im, powers[-1], power))
        power_ref[i] = power


def last_finish_kernel(own_ref, above_ref, below_ref, power_ref, out_ref):
    for i in range(own_ref.shape[1]):
        power, re, im = (whole_sum(own_ref, above_ref, below_ref, n, i) for n in range(3))
        deal(out_ref, i * TALL, coherence(re, im, power_ref[i], power))


def settle_kernel(*refs):
    out_ref = refs[-1]
    base = 0
    for got_ref in refs[:-1]:
        group = got_ref.shape[0]
        tall = out_ref.shape[1] // (TALL * group)
        pairs = got_ref.shape[1] // (tall * TALL)
        for device in range(group):
            strip = strip_of(device, group)
            for k in range(pairs):
                for i in range(tall):
                    for r in range(TALL):
                        at = (k * tall + i) * TALL + r
                        row = (r * group + strip) * tall + i
                        out_ref[base + k, row : row + 1] = got_ref[device, at : at + 1]
        base += pairs


def local(radar_subimages, owning_sector, sector_down_start, sector_across_start):
    group = lax.axis_size("grid")
    held, dates, planes, side, _ = radar_subimages.shape
    rows = side // group
    lines = group * TALL
    cols = WIDE * side
    span = dates - 2
    me = lax.axis_index("grid").astype(jnp.int32)
    devices = jnp.arange(group, dtype=jnp.int32)
    at = device_at(group)
    cells = radar_subimages.reshape(held, dates, planes, group, rows, side)
    cells = pltpu.with_memory_space_constraint(cells, pltpu.HBM)

    words = [
        pltpu.with_memory_space_constraint(word.reshape(1, held), pltpu.HBM)
        for word in (owning_sector, sector_down_start, sector_across_start)
    ]
    bulk = bulk_cut(*words, cells, span)
    got = lax.all_to_all(bulk, "grid", split_axis=0, concat_axis=0, tiled=True)
    strips = strip_of(me ^ devices, group)

    def scatter(date, after=None):
        sends = cut(strips, cells, date)
        if after is not None:
            sends, _ = lax.optimization_barrier((sends, after))
        pieces = [sends[0]] + [None] * (group - 1)
        for m in range(1, group):
            pieces[m] = lax.ppermute(sends[m], "grid", [(i, i ^ m) for i in range(group)])
        return pieces

    pieces_b = scatter(dates - 2)
    pieces = scatter(dates - 1, got if LATE else None)

    col = jnp.arange(cols)[:, None]
    out_col = jnp.arange(cols // 4)[None, :]
    window = ((col >= 4 * out_col - 12) & (col <= 4 * out_col + 15)).astype(jnp.bfloat16)
    tags = got[:, -1, :2, :held].astype(jnp.int32)
    places = tags[:, 1] * lines + tags[:, 0]
    flat = places.reshape(group * held)
    counts = jnp.sum((flat[:, None] == flat[None, :]).astype(jnp.int32), axis=1)
    shares = 1.0 / jnp.maximum(counts, 1).astype(jnp.float32)
    tables = (flat, shares)
    swapped = tuple(t.reshape(group, held)[me ^ devices].reshape(group * held) for t in tables)

    def exchange(up, down):
        below = lax.ppermute(up, "grid", [(at[s], at[s - 1]) for s in range(group)])
        above = lax.ppermute(down, "grid", [(at[s - 1], at[s]) for s in range(group)])
        return above, below

    comp = pltpu.VMEM((lines * WIDE, planes, rows, side), jnp.float32)
    out_cols = cols // 4
    tall = rows // 4
    outs, sums = sums_of(3 * span - 2, rows, lines, out_cols)
    kept, own, up, down = call(
        functools.partial(bulk_step_kernel, group=group, held=held),
        (strips, *tables), (got, window), [comp, *outs], [sums] + [comp] * (span - 1),
        mib=32,
    )
    above, below = exchange(up, down)
    outs, sums = sums_of(3, rows, lines, out_cols)
    kept, *next_sums = call(
        functools.partial(step_kernel, group=group, held=held),
        (strips, *swapped), (*pieces_b, window, kept), [comp, *outs], [sums],
    )
    next_own, up, down = next_sums
    next_above, next_below = exchange(up, down)
    dealt, power = call(
        functools.partial(bulk_finish_kernel, span=span), (),
        (own, above, below, next_own, next_above, next_below),
        [
            jax.ShapeDtypeStruct((group, span * tall * TALL, out_cols), jnp.float32),
            jax.ShapeDtypeStruct((tall, lines, out_cols), jnp.float32),
        ],
    )
    if LATE:
        first = lax.all_to_all(dealt, "grid", split_axis=0, concat_axis=0, tiled=True)

    near = group // 2
    (part,) = call(functools.partial(part_kernel, base=0, held=held), swapped, pieces[:near], [comp])
    far = pieces[near:]
    _, own, up, down = call(
        functools.partial(last_step_kernel, group=group, base=near, held=held),
        (strips, *swapped), (*far, window, kept, part), [comp, *outs], [sums], aliases={3 + len(far) + 2: 0},
    )
    above, below = exchange(up, down)
    (last,) = call(
        last_finish_kernel, (), (own, above, below, power),
        [jax.ShapeDtypeStruct((group, tall * TALL, out_cols), jnp.float32)],
    )
    if LATE:
        second = lax.all_to_all(last, "grid", split_axis=0, concat_axis=0, tiled=True)
        got = (first, second)
    else:
        last = jnp.concatenate([dealt, last], axis=1)
        got = (lax.all_to_all(last, "grid", split_axis=0, concat_axis=0, tiled=True),)
    (out,) = call(
        settle_kernel, (), got,
        [jax.ShapeDtypeStruct((dates - 1, TALL * side // 4, out_cols), jnp.float32)],
    )
    return out


def solution(mesh):
    in_specs = (
        P(("region", "grid"), None, None, None, None),
        P(("region", "grid"), None),
        P(("region", "grid")),
        P(("region", "grid")),
    )
    out_specs = P(None, ("region", "grid"), None)

    return jax.shard_map(local, mesh=mesh, in_specs=in_specs, out_specs=out_specs, check_vma=False)
```

```python
import functools

import jax
import jax.numpy as jnp
from jax import lax
from jax.experimental import pallas as pl
from jax.experimental.pallas import tpu as pltpu
from jax.sharding import PartitionSpec as P


TALL = 4
WIDE = 8
EPSILON = 1e-06
LATE = False
LANES = 128
VMEM = pl.BlockSpec(memory_space=pltpu.VMEM)
HBM = pl.BlockSpec(memory_space=pltpu.HBM)


def strip_of(device, group):
    if group % 4:
        return device
    column, side, core = device // 4, (device // 2) % 2, device % 2
    return side * (group // 2) + 2 * (column + side * (group // 4 - 1 - 2 * column)) + core


def shifted(device, m, group, sign=1):
    if group % 4:
        return (device + sign * m) % group
    return ((device // 4 + sign * (m // 4)) % (group // 4)) * 4 + ((device % 4) ^ (m % 4))


def started(group):
    steps = group // 4 if group % 4 == 0 else group
    width = group // steps
    half = steps // 2
    order = [c for n in range(1, half) for c in (steps - n, n)]
    order += [c for c in range(1, steps) if c not in order]
    ahead = [m for c in order[:-1] for m in range(c * width, (c + 1) * width)]
    return ahead, list(range(1, width)), list(range(order[-1] * width, (order[-1] + 1) * width))


def device_at(group):
    places = [strip_of(d, group) for d in range(group)]
    return [places.index(s) for s in range(group)]


def bulk_kernel(*refs, span):
    words, (cells_ref, out_ref, *bufs, in_buf, out_buf, tag_buf, word_sem, in_sem, out_sem) = refs[:3], refs[3:]
    parts, each = in_buf.shape[:2]
    group, _, rows, side = out_buf.shape
    planes = in_buf.shape[3]
    held = parts * each
    many = each * span * planes
    fetches = [
        pltpu.make_async_copy(cells_ref.at[pl.ds(j * each, each), pl.ds(0, span)], in_buf.at[j], in_sem.at[j])
        for j in range(parts)
    ]
    small = [pltpu.make_async_copy(word, buf, word_sem.at[n]) for n, (word, buf) in enumerate(zip(words, bufs))]
    for fetch in small + fetches:
        fetch.start()
    for fetch in small:
        fetch.wait()
    owner_ref, down_ref, across_ref = bufs
    tag_buf[...] = jnp.zeros(tag_buf.shape, jnp.float32)
    tag_buf[0:1, :held] = (owner_ref[...] * TALL + down_ref[...]).astype(jnp.float32)
    tag_buf[1:2, :held] = across_ref[...].astype(jnp.float32)
    tag = tag_buf[...].astype(out_buf.dtype)
    stores = []
    for j, fetch in enumerate(fetches):
        fetch.wait()
        more = j == parts - 1
        for g in range(group):
            strip = strip_of(g, group)
            out_buf[g, j * many : (j + 1) * many] = in_buf[j, :, :, :, strip].reshape(many, rows, side)
            if more:
                out_buf[g, held * span * planes] = tag
            piece = pl.ds(j * many, many + more)
            stores.append(pltpu.make_async_copy(out_buf.at[g, piece], out_ref.at[g, piece], out_sem.at[j, g]))
            stores[-1].start()
    for store in stores:
        store.wait()


def bulk_cut(owner, down, across, cells, span):
    held, _, planes, group, rows, side = cells.shape
    parts = next(p for p in (4, 3, 2, 1) if held % p == 0)
    out = jax.ShapeDtypeStruct((group, held * span * planes + 1, rows, side), cells.dtype)
    return pl.pallas_call(
        functools.partial(bulk_kernel, span=span),
        out_shape=pltpu.HBM(out.shape, out.dtype),
        in_specs=[HBM] * 4,
        out_specs=HBM,
        scratch_shapes=[
            *[pltpu.VMEM((1, held), jnp.int32)] * 3,
            pltpu.VMEM((parts, held // parts, span, planes, group, rows, side), cells.dtype),
            pltpu.VMEM(out.shape, out.dtype),
            pltpu.VMEM((rows, side), jnp.float32),
            pltpu.SemaphoreType.DMA((3,)),
            pltpu.SemaphoreType.DMA((parts,)),
            pltpu.SemaphoreType.DMA((parts, group)),
        ],
        compiler_params=pltpu.CompilerParams(vmem_limit_bytes=12 << 20),
        name="bulk_cut",
    )(owner, down, across, cells)


def cut_kernel(strip_ref, cells_ref, *outs):
    held, _, planes, _, rows, side = cells_ref.shape
    for m, out in enumerate(outs):
        out[...] = cells_ref[:, 0, :, strip_ref[m]].reshape(held * planes, rows, side)


def cut(strips, cells, date):
    held, _, planes, group, rows, side = cells.shape
    piece = (held * planes, rows, side)
    return pl.pallas_call(
        cut_kernel,
        out_shape=[pltpu.HBM(piece, cells.dtype)] * group,
        grid_spec=pltpu.PrefetchScalarGridSpec(
            num_scalar_prefetch=1,
            grid=(1,),
            in_specs=[pl.BlockSpec((held, 1, planes, group, rows, side), lambda i, strips: (0, date, 0, 0, 0, 0))],
            out_specs=[pl.BlockSpec(piece, lambda i, strips: (0, 0, 0))] * group,
        ),
        compiler_params=pltpu.CompilerParams(vmem_limit_bytes=10 << 20),
        name="cut",
    )(strips, cells)


def gather(place_ref, share_ref, pieces, fetches, comps, names, held):
    span, planes = len(comps), comps[0].shape[1]
    for name, piece, fetch in zip(names, pieces, fetches):
        fetch.wait()

        def add(k, carry, name=name, piece=piece):
            place = place_ref[name * held + k]
            share = share_ref[name * held + k]
            for d, comp in enumerate(comps):
                for q in range(planes):
                    comp[place, q] += piece[(k * span + d) * planes + q].astype(jnp.float32) * share
            return carry

        lax.fori_loop(0, held, add, 0, unroll=4)


def start_all(sources, buf_ref, sems):
    fetches = [pltpu.make_async_copy(source, buf_ref.at[m], sems.at[m]) for m, source in enumerate(sources)]
    for fetch in fetches:
        fetch.start()
    return [buf_ref.at[m] for m in range(len(sources))], fetches


def box_sums(strip, comps, window_ref, window_copy, sums_ref, own_ref, up_ref, down_ref, group, skip):
    slots, _, rows, side = comps[0].shape
    lines = slots // WIDE
    step = min(lines, 16)
    window_copy.wait()
    window = window_ref[...]

    def row_of(comp, q, at):
        parts = [comp[pl.ds(c * lines + at, step), q].reshape(step * rows, side) for c in range(WIDE)]
        return jnp.concatenate(parts, axis=1)

    def emit(index, field, at):
        high = field.astype(jnp.bfloat16)
        low = (field - high.astype(jnp.float32)).astype(jnp.bfloat16)
        total = jnp.dot(high, window, preferred_element_type=jnp.float32)
        total += jnp.dot(low, window, preferred_element_type=jnp.float32)
        for half in range(sums_ref.shape[1]):
            sums_ref[index, half, pl.ds(at * rows, step * rows), :] = total[:, half * LANES : (half + 1) * LANES]

    for number in range(lines // step):
        at = number * step
        index = 0
        re_old = im_old = None
        for d, comp in enumerate(comps):
            re, im = row_of(comp, 0, at), row_of(comp, 1, at)
            if d >= skip:
                emit(index, re * re + im * im, at)
                index += 1
            if d:
                emit(index, re_old * re + im_old * im, at)
                emit(index + 1, im_old * re - re_old * im, at)
                index += 2
            re_old, im_old = re, im
    for f in range(sums_ref.shape[0]):
        level = [
            jnp.concatenate(
                [sums_ref[f, half, pl.ds(y, lines, stride=rows), :] for half in range(sums_ref.shape[1])], axis=1
            )
            for y in range(rows)
        ]
        for i in range(rows // 4):
            begin, end = max(0, 4 * i - 1), min(rows, 4 * i + 6)
            own_ref[f, i] = sum(level[begin + 1 : end], level[begin])
        up, down = level[0] + level[1], level[rows - 1]
        line = lax.broadcasted_iota(jnp.int32, up.shape, 0)
        up_next = jnp.where(line == lines - 1, 0.0, pltpu.roll(up, lines - 1, 0))
        down_next = jnp.where(line == 0, 0.0, pltpu.roll(down, 1, 0))
        up_ref[f] = jnp.where(strip == 0, up_next, up)
        down_ref[f] = jnp.where(strip == group - 1, down_next, down)


def begin(window_hbm, window_ref, window_sem, sources, buf_ref, sems, comps):
    views, fetches = start_all(sources, buf_ref, sems)
    window_copy = pltpu.make_async_copy(window_hbm, window_ref, window_sem)
    window_copy.start()
    for comp in comps:
        comp[...] = jnp.zeros(comp.shape, jnp.float32)
    return views, fetches, window_copy


def bulk_step_kernel(strip_ref, place_ref, share_ref, got_ref, window_hbm, kept_ref, own_ref, up_ref, down_ref, *scratch, group, held):
    window_ref, window_sem, buf_ref, sems, sums_ref, *fresh = scratch
    comps = [*fresh, kept_ref]
    sources = [got_ref.at[m] for m in range(group)]
    views, fetches, window_copy = begin(window_hbm, window_ref, window_sem, sources, buf_ref, sems, comps)
    gather(place_ref, share_ref, views, fetches, comps, range(group), held)
    box_sums(strip_ref[0], comps, window_ref, window_copy, sums_ref, own_ref, up_ref, down_ref, group, 0)


def step_kernel(strip_ref, place_ref, share_ref, *refs, group, held):
    pieces, (window_hbm, before_ref, comp, own_ref, up_ref, down_ref) = refs[:group], refs[group : group + 6]
    window_ref, window_sem, buf_ref, sems, sums_ref = refs[group + 6 :]
    views, fetches, window_copy = begin(window_hbm, window_ref, window_sem, pieces, buf_ref, sems, [comp])
    gather(place_ref, share_ref, views, fetches, [comp], range(group), held)
    box_sums(strip_ref[0], [before_ref, comp], window_ref, window_copy, sums_ref, own_ref, up_ref, down_ref, group, 1)


def part_kernel(place_ref, share_ref, *refs, names, held):
    pieces, (*old, comp, buf_ref, sems) = refs[: len(names)], refs[len(names) :]
    views, fetches = start_all(pieces, buf_ref, sems)
    if not old:
        comp[...] = jnp.zeros(comp.shape, jnp.float32)
    gather(place_ref, share_ref, views, fetches, [comp], names, held)


def last_step_kernel(strip_ref, place_ref, share_ref, *refs, group, names, held):
    many = len(names)
    pieces, (window_hbm, before_ref, _, comp, own_ref, up_ref, down_ref) = refs[:many], refs[many : many + 7]
    window_ref, window_sem, buf_ref, sems, sums_ref = refs[many + 7 :]
    views, fetches, window_copy = begin(window_hbm, window_ref, window_sem, pieces, buf_ref, sems, [])
    gather(place_ref, share_ref, views, fetches, [comp], names, held)
    box_sums(strip_ref[0], [before_ref, comp], window_ref, window_copy, sums_ref, own_ref, up_ref, down_ref, group, 1)


def sums_of(fields, rows, lines, cols):
    outs = [(fields, rows // 4, lines, cols), (fields, lines, cols), (fields, lines, cols)]
    return [jax.ShapeDtypeStruct(s, jnp.float32) for s in outs], pltpu.VMEM((fields, cols // LANES, lines * rows, LANES), jnp.float32)


def call(kernel, prefetch, args, outs, scratch=(), aliases=None, mib=12, remote=0):
    return pl.pallas_call(
        kernel,
        out_shape=outs,
        grid_spec=pltpu.PrefetchScalarGridSpec(
            num_scalar_prefetch=len(prefetch),
            grid=(),
            in_specs=[HBM] * remote + [VMEM] * (len(args) - remote),
            out_specs=[VMEM] * len(outs),
            scratch_shapes=list(scratch),
        ),
        input_output_aliases=aliases or {},
        compiler_params=pltpu.CompilerParams(vmem_limit_bytes=mib << 20),
    )(*prefetch, *args)


def whole_sum(own_ref, above_ref, below_ref, f, i):
    total = own_ref[f, i]
    if i == 0:
        total = total + above_ref[f]
    if i == own_ref.shape[1] - 1:
        total = total + below_ref[f]
    return total


def coherence(re, im, first, second):
    return jnp.sqrt(re * re + im * im) / jnp.sqrt(first * second + EPSILON)


def deal(out_ref, at, value):
    for g in range(out_ref.shape[0]):
        out_ref[g, at : at + TALL] = value[g * TALL : (g + 1) * TALL]


def bulk_finish_kernel(own_ref, above_ref, below_ref, next_ref, next_above_ref, next_below_ref, out_ref, power_ref, *, span):
    tall = own_ref.shape[1]
    for i in range(tall):
        powers = []
        for d in range(span):
            at = 0 if d == 0 else 3 * d - 2
            powers.append(whole_sum(own_ref, above_ref, below_ref, at, i))
            if d:
                re, im = (whole_sum(own_ref, above_ref, below_ref, at + n, i) for n in (1, 2))
                deal(out_ref, ((d - 1) * tall + i) * TALL, coherence(re, im, powers[-2], powers[-1]))
        power, re, im = (whole_sum(next_ref, next_above_ref, next_below_ref, n, i) for n in range(3))
        deal(out_ref, ((span - 1) * tall + i) * TALL, coherence(re, im, powers[-1], power))
        power_ref[i] = power


def last_finish_kernel(own_ref, above_ref, below_ref, power_ref, out_ref):
    for i in range(own_ref.shape[1]):
        power, re, im = (whole_sum(own_ref, above_ref, below_ref, n, i) for n in range(3))
        deal(out_ref, i * TALL, coherence(re, im, power_ref[i], power))


def settle_kernel(*refs):
    out_ref = refs[-1]
    base = 0
    for got_ref in refs[:-1]:
        group = got_ref.shape[0]
        tall = out_ref.shape[1] // (TALL * group)
        pairs = got_ref.shape[1] // (tall * TALL)
        for device in range(group):
            strip = strip_of(device, group)
            for k in range(pairs):
                for i in range(tall):
                    for r in range(TALL):
                        at = (k * tall + i) * TALL + r
                        row = (r * group + strip) * tall + i
                        out_ref[base + k, row : row + 1] = got_ref[device, at : at + 1]
        base += pairs


def local(radar_subimages, owning_sector, sector_down_start, sector_across_start):
    group = lax.axis_size("grid")
    held, dates, planes, side, _ = radar_subimages.shape
    rows = side // group
    lines = group * TALL
    cols = WIDE * side
    span = dates - 2
    me = lax.axis_index("grid").astype(jnp.int32)
    devices = jnp.arange(group, dtype=jnp.int32)
    at = device_at(group)
    cells = radar_subimages.reshape(held, dates, planes, group, rows, side)
    cells = pltpu.with_memory_space_constraint(cells, pltpu.HBM)

    words = [
        pltpu.with_memory_space_constraint(word.reshape(1, held), pltpu.HBM)
        for word in (owning_sector, sector_down_start, sector_across_start)
    ]
    bulk = bulk_cut(*words, cells, span)
    got = lax.all_to_all(bulk, "grid", split_axis=0, concat_axis=0, tiled=True)
    strips = strip_of(shifted(me, devices, group), group)

    def scatter(date, after=None):
        sends = cut(strips, cells, date)
        if after is not None:
            sends, _ = lax.optimization_barrier((sends, after))
        pieces = [sends[0]] + [None] * (group - 1)
        for m in range(1, group):
            pieces[m] = lax.ppermute(sends[m], "grid", [(i, shifted(i, m, group)) for i in range(group)])
        return pieces

    pieces_b = scatter(dates - 2)
    pieces = scatter(dates - 1, got if LATE else None)

    col = jnp.arange(cols)[:, None]
    out_col = jnp.arange(cols // 4)[None, :]
    window = ((col >= 4 * out_col - 12) & (col <= 4 * out_col + 15)).astype(jnp.bfloat16)
    tags = got[:, -1, :2, :held].astype(jnp.int32)
    places = tags[:, 1] * lines + tags[:, 0]
    flat = places.reshape(group * held)
    counts = jnp.sum((flat[:, None] == flat[None, :]).astype(jnp.int32), axis=1)
    shares = 1.0 / jnp.maximum(counts, 1).astype(jnp.float32)
    tables = (flat, shares)
    swapped = tuple(t.reshape(group, held)[shifted(me, devices, group, -1)].reshape(group * held) for t in tables)
    tables, swapped = lax.optimization_barrier((tables, swapped))

    def exchange(up, down):
        below = lax.ppermute(up, "grid", [(at[s], at[s - 1]) for s in range(group)])
        above = lax.ppermute(down, "grid", [(at[s - 1], at[s]) for s in range(group)])
        return above, below

    window_bufs = [pltpu.VMEM(window.shape, window.dtype), pltpu.SemaphoreType.DMA(())]

    def piece_bufs(many):
        return [pltpu.VMEM((many, *pieces[0].shape), pieces[0].dtype), pltpu.SemaphoreType.DMA((many,))]

    comp = pltpu.VMEM((lines * WIDE, planes, rows, side), jnp.float32)
    out_cols = cols // 4
    tall = rows // 4
    outs, sums = sums_of(3 * span - 2, rows, lines, out_cols)
    kept, own, up, down = call(
        functools.partial(bulk_step_kernel, group=group, held=held),
        (strips, *tables), (got, window), [comp, *outs],
        [*window_bufs, pltpu.VMEM(got.shape, got.dtype), pltpu.SemaphoreType.DMA((group,)), sums] + [comp] * (span - 1),
        mib=16, remote=2,
    )
    above, below = exchange(up, down)
    outs, sums = sums_of(3, rows, lines, out_cols)
    kept, *next_sums = call(
        functools.partial(step_kernel, group=group, held=held),
        (strips, *swapped), (*pieces_b, window, kept), [comp, *outs],
        [*window_bufs, *piece_bufs(group), sums], remote=group + 1,
    )
    next_own, up, down = next_sums
    next_above, next_below = exchange(up, down)
    dealt, power = call(
        functools.partial(bulk_finish_kernel, span=span), (),
        (own, above, below, next_own, next_above, next_below),
        [
            jax.ShapeDtypeStruct((group, span * tall * TALL, out_cols), jnp.float32),
            jax.ShapeDtypeStruct((tall, lines, out_cols), jnp.float32),
        ],
    )
    if LATE:
        first = lax.all_to_all(dealt, "grid", split_axis=0, concat_axis=0, tiled=True)

    ahead, level, late = started(group)
    near, middle, far = [0, *level, *ahead[: len(ahead) // 2]], ahead[len(ahead) // 2 :], late
    (part,) = call(
        functools.partial(part_kernel, names=near, held=held), swapped, [pieces[m] for m in near], [comp],
        piece_bufs(len(near)), remote=len(near),
    )
    (part,) = call(
        functools.partial(part_kernel, names=middle, held=held), swapped, (*[pieces[m] for m in middle], part), [comp],
        piece_bufs(len(middle)), aliases={2 + len(middle): 0}, remote=len(middle),
    )
    far_pieces = [pieces[m] for m in far]
    _, own, up, down = call(
        functools.partial(last_step_kernel, group=group, names=far, held=held),
        (strips, *swapped), (*far_pieces, window, kept, part), [comp, *outs],
        [*window_bufs, *piece_bufs(len(far)), sums], aliases={3 + len(far) + 2: 0},
        remote=len(far) + 1,
    )
    above, below = exchange(up, down)
    (last,) = call(
        last_finish_kernel, (), (own, above, below, power),
        [jax.ShapeDtypeStruct((group, tall * TALL, out_cols), jnp.float32)],
    )
    if LATE:
        second = lax.all_to_all(last, "grid", split_axis=0, concat_axis=0, tiled=True)
        got = (first, second)
    else:
        last = jnp.concatenate([dealt, last], axis=1)
        got = (lax.all_to_all(last, "grid", split_axis=0, concat_axis=0, tiled=True),)
    (out,) = call(
        settle_kernel, (), got,
        [jax.ShapeDtypeStruct((dates - 1, TALL * side // 4, out_cols), jnp.float32)],
    )
    return out


def solution(mesh):
    in_specs = (
        P(("region", "grid"), None, None, None, None),
        P(("region", "grid"), None),
        P(("region", "grid")),
        P(("region", "grid")),
    )
    out_specs = P(None, ("region", "grid"), None)

    return jax.shard_map(local, mesh=mesh, in_specs=in_specs, out_specs=out_specs, check_vma=False)
```

```python
import functools

import jax
import jax.numpy as jnp
from jax import lax
from jax.experimental import pallas as pl
from jax.experimental.pallas import tpu as pltpu
from jax.sharding import PartitionSpec as P


TALL = 4
WIDE = 8
EPSILON = 1e-06
LANES = 128
VMEM = pl.BlockSpec(memory_space=pltpu.VMEM)
HBM = pl.BlockSpec(memory_space=pltpu.HBM)


def strip_of(device, group):
    if group % 4:
        return device
    column, side, core = device // 4, (device // 2) % 2, device % 2
    return side * (group // 2) + 2 * (column + side * (group // 4 - 1 - 2 * column)) + core


def shifted(device, m, group, sign=1):
    if group % 4:
        return (device + sign * m) % group
    return ((device // 4 + sign * (m // 4)) % (group // 4)) * 4 + ((device % 4) ^ (m % 4))


def started(group):
    steps = group // 4 if group % 4 == 0 else group
    width = group // steps
    half = steps // 2
    order = [c for n in range(1, half) for c in (steps - n, n)]
    order += [c for c in range(1, steps) if c not in order]
    ahead = [m for c in order[:-1] for m in range(c * width, (c + 1) * width)]
    return ahead, list(range(1, width)), list(range(order[-1] * width, (order[-1] + 1) * width))


def device_at(group):
    places = [strip_of(d, group) for d in range(group)]
    return [places.index(s) for s in range(group)]


def bulk_kernel(*refs, span):
    words, (cells_ref, out_ref, *bufs, in_buf, out_buf, tag_buf, word_sem, in_sem, out_sem) = refs[:3], refs[3:]
    parts, each = in_buf.shape[:2]
    group, _, rows, side = out_buf.shape
    planes = in_buf.shape[3]
    held = parts * each
    many = each * span * planes
    fetches = [
        pltpu.make_async_copy(cells_ref.at[pl.ds(j * each, each), pl.ds(0, span)], in_buf.at[j], in_sem.at[j])
        for j in range(parts)
    ]
    small = [pltpu.make_async_copy(word, buf, word_sem.at[n]) for n, (word, buf) in enumerate(zip(words, bufs))]
    for fetch in small + fetches:
        fetch.start()
    stores = []
    for j, fetch in enumerate(fetches):
        fetch.wait()
        more = j == parts - 1
        if more:
            for copy in small:
                copy.wait()
            owner_ref, down_ref, across_ref = bufs
            tag_buf[...] = jnp.zeros(tag_buf.shape, jnp.float32)
            tag_buf[0:1, :held] = (owner_ref[...] * TALL + down_ref[...]).astype(jnp.float32)
            tag_buf[1:2, :held] = across_ref[...].astype(jnp.float32)
            tag = tag_buf[...].astype(out_buf.dtype)
        for g in range(group):
            strip = strip_of(g, group)
            out_buf[g, j * many : (j + 1) * many] = in_buf[j, :, :, :, strip].reshape(many, rows, side)
            if more:
                out_buf[g, held * span * planes] = tag
            piece = pl.ds(j * many, many + more)
            stores.append(pltpu.make_async_copy(out_buf.at[g, piece], out_ref.at[g, piece], out_sem.at[j, g]))
            stores[-1].start()
    for store in stores:
        store.wait()


def bulk_cut(owner, down, across, cells, span):
    held, _, planes, group, rows, side = cells.shape
    parts = next(p for p in (6, 4, 3, 2, 1) if held % p == 0)
    out = jax.ShapeDtypeStruct((group, held * span * planes + 1, rows, side), cells.dtype)
    return pl.pallas_call(
        functools.partial(bulk_kernel, span=span),
        out_shape=pltpu.HBM(out.shape, out.dtype),
        in_specs=[HBM] * 4,
        out_specs=HBM,
        scratch_shapes=[
            *[pltpu.VMEM((1, held), jnp.int32)] * 3,
            pltpu.VMEM((parts, held // parts, span, planes, group, rows, side), cells.dtype),
            pltpu.VMEM(out.shape, out.dtype),
            pltpu.VMEM((rows, side), jnp.float32),
            pltpu.SemaphoreType.DMA((3,)),
            pltpu.SemaphoreType.DMA((parts,)),
            pltpu.SemaphoreType.DMA((parts, group)),
        ],
        compiler_params=pltpu.CompilerParams(vmem_limit_bytes=12 << 20),
        name="bulk_cut",
    )(owner, down, across, cells)


def cut_kernel(strip_ref, cells_ref, *outs):
    held, _, planes, _, rows, side = cells_ref.shape
    for m, out in enumerate(outs):
        out[...] = cells_ref[:, 0, :, strip_ref[m]].reshape(held * planes, rows, side)


def cut(strips, cells, date):
    held, _, planes, group, rows, side = cells.shape
    piece = (held * planes, rows, side)
    return pl.pallas_call(
        cut_kernel,
        out_shape=[pltpu.HBM(piece, cells.dtype)] * group,
        grid_spec=pltpu.PrefetchScalarGridSpec(
            num_scalar_prefetch=1,
            grid=(1,),
            in_specs=[pl.BlockSpec((held, 1, planes, group, rows, side), lambda i, strips: (0, date, 0, 0, 0, 0))],
            out_specs=[pl.BlockSpec(piece, lambda i, strips: (0, 0, 0))] * group,
        ),
        compiler_params=pltpu.CompilerParams(vmem_limit_bytes=10 << 20),
        name="cut",
    )(strips, cells)


def gather(place_ref, share_ref, pieces, fetches, comps, names, held):
    span, planes = len(comps), comps[0].shape[1]
    for name, piece, fetch in zip(names, pieces, fetches):
        fetch.wait()

        def add(k, carry, name=name, piece=piece):
            place = place_ref[name * held + k]
            share = share_ref[name * held + k]
            for d, comp in enumerate(comps):
                for q in range(planes):
                    comp[place, q] += piece[(k * span + d) * planes + q].astype(jnp.float32) * share
            return carry

        lax.fori_loop(0, held, add, 0, unroll=4)


def start_all(sources, buf_ref, sems):
    fetches = [pltpu.make_async_copy(source, buf_ref.at[m], sems.at[m]) for m, source in enumerate(sources)]
    for fetch in fetches:
        fetch.start()
    return [buf_ref.at[m] for m in range(len(sources))], fetches


def box_sums(strip, comps, window_ref, window_copy, sums_ref, own_ref, up_ref, down_ref, group, skip):
    slots, _, rows, side = comps[0].shape
    lines = slots // WIDE
    step = min(lines, 16)
    window_copy.wait()
    window = window_ref[...]

    def row_of(comp, q, at):
        parts = [comp[pl.ds(c * lines + at, step), q].reshape(step * rows, side) for c in range(WIDE)]
        return jnp.concatenate(parts, axis=1)

    def emit(index, field, at):
        high = field.astype(jnp.bfloat16)
        low = (field - high.astype(jnp.float32)).astype(jnp.bfloat16)
        total = jnp.dot(high, window, preferred_element_type=jnp.float32)
        total += jnp.dot(low, window, preferred_element_type=jnp.float32)
        for half in range(sums_ref.shape[1]):
            sums_ref[index, half, pl.ds(at * rows, step * rows), :] = total[:, half * LANES : (half + 1) * LANES]

    for number in range(lines // step):
        at = number * step
        index = 0
        re_old = im_old = None
        for d, comp in enumerate(comps):
            re, im = row_of(comp, 0, at), row_of(comp, 1, at)
            if d >= skip:
                emit(index, re * re + im * im, at)
                index += 1
            if d:
                emit(index, re_old * re + im_old * im, at)
                emit(index + 1, im_old * re - re_old * im, at)
                index += 2
            re_old, im_old = re, im
    for f in range(sums_ref.shape[0]):
        level = [
            jnp.concatenate(
                [sums_ref[f, half, pl.ds(y, lines, stride=rows), :] for half in range(sums_ref.shape[1])], axis=1
            )
            for y in range(rows)
        ]
        for i in range(rows // 4):
            begin, end = max(0, 4 * i - 1), min(rows, 4 * i + 6)
            own_ref[f, i] = sum(level[begin + 1 : end], level[begin])
        up, down = level[0] + level[1], level[rows - 1]
        line = lax.broadcasted_iota(jnp.int32, up.shape, 0)
        up_next = jnp.where(line == lines - 1, 0.0, pltpu.roll(up, lines - 1, 0))
        down_next = jnp.where(line == 0, 0.0, pltpu.roll(down, 1, 0))
        up_ref[f] = jnp.where(strip == 0, up_next, up)
        down_ref[f] = jnp.where(strip == group - 1, down_next, down)


def begin(window_hbm, window_ref, window_sem, sources, buf_ref, sems, comps):
    views, fetches = start_all(sources, buf_ref, sems)
    window_copy = pltpu.make_async_copy(window_hbm, window_ref, window_sem)
    window_copy.start()
    for comp in comps:
        comp[...] = jnp.zeros(comp.shape, jnp.float32)
    return views, fetches, window_copy


def bulk_step_kernel(strip_ref, place_ref, share_ref, got_ref, window_hbm, kept_ref, own_ref, up_ref, down_ref, *scratch, group, held):
    window_ref, window_sem, buf_ref, sems, sums_ref, *fresh = scratch
    comps = [*fresh, kept_ref]
    sources = [got_ref.at[m] for m in range(group)]
    views, fetches, window_copy = begin(window_hbm, window_ref, window_sem, sources, buf_ref, sems, comps)
    gather(place_ref, share_ref, views, fetches, comps, range(group), held)
    box_sums(strip_ref[0], comps, window_ref, window_copy, sums_ref, own_ref, up_ref, down_ref, group, 0)


def step_kernel(strip_ref, place_ref, share_ref, *refs, group, held):
    pieces, (window_hbm, before_ref, comp, own_ref, up_ref, down_ref) = refs[:group], refs[group : group + 6]
    window_ref, window_sem, buf_ref, sems, sums_ref = refs[group + 6 :]
    views, fetches, window_copy = begin(window_hbm, window_ref, window_sem, pieces, buf_ref, sems, [comp])
    gather(place_ref, share_ref, views, fetches, [comp], range(group), held)
    box_sums(strip_ref[0], [before_ref, comp], window_ref, window_copy, sums_ref, own_ref, up_ref, down_ref, group, 1)


def part_kernel(place_ref, share_ref, *refs, names, held):
    pieces, (*old, comp, buf_ref, sems) = refs[: len(names)], refs[len(names) :]
    views, fetches = start_all(pieces, buf_ref, sems)
    if not old:
        comp[...] = jnp.zeros(comp.shape, jnp.float32)
    gather(place_ref, share_ref, views, fetches, [comp], names, held)


def last_step_kernel(strip_ref, place_ref, share_ref, *refs, group, names, held):
    many = len(names)
    pieces, (window_hbm, before_ref, _, comp, own_ref, up_ref, down_ref) = refs[:many], refs[many : many + 7]
    window_ref, window_sem, buf_ref, sems, sums_ref = refs[many + 7 :]
    views, fetches, window_copy = begin(window_hbm, window_ref, window_sem, pieces, buf_ref, sems, [])
    gather(place_ref, share_ref, views, fetches, [comp], names, held)
    box_sums(strip_ref[0], [before_ref, comp], window_ref, window_copy, sums_ref, own_ref, up_ref, down_ref, group, 1)


def sums_of(fields, rows, lines, cols):
    outs = [(fields, rows // 4, lines, cols), (fields, lines, cols), (fields, lines, cols)]
    return [jax.ShapeDtypeStruct(s, jnp.float32) for s in outs], pltpu.VMEM((fields, cols // LANES, lines * rows, LANES), jnp.float32)


def call(kernel, prefetch, args, outs, scratch=(), aliases=None, mib=12, remote=0):
    return pl.pallas_call(
        kernel,
        out_shape=outs,
        grid_spec=pltpu.PrefetchScalarGridSpec(
            num_scalar_prefetch=len(prefetch),
            grid=(),
            in_specs=[HBM] * remote + [VMEM] * (len(args) - remote),
            out_specs=[VMEM] * len(outs),
            scratch_shapes=list(scratch),
        ),
        input_output_aliases=aliases or {},
        compiler_params=pltpu.CompilerParams(vmem_limit_bytes=mib << 20),
    )(*prefetch, *args)


def whole_sum(own_ref, above_ref, below_ref, f, i):
    total = own_ref[f, i]
    if i == 0:
        total = total + above_ref[f]
    if i == own_ref.shape[1] - 1:
        total = total + below_ref[f]
    return total


def coherence(re, im, first, second):
    return jnp.sqrt(re * re + im * im) / jnp.sqrt(first * second + EPSILON)


def deal(out_ref, at, value):
    for g in range(out_ref.shape[0]):
        out_ref[g, at : at + TALL] = value[g * TALL : (g + 1) * TALL]


def bulk_finish_kernel(own_ref, above_ref, below_ref, next_ref, next_above_ref, next_below_ref, out_ref, power_ref, *, span):
    tall = own_ref.shape[1]
    for i in range(tall):
        powers = []
        for d in range(span):
            at = 0 if d == 0 else 3 * d - 2
            powers.append(whole_sum(own_ref, above_ref, below_ref, at, i))
            if d:
                re, im = (whole_sum(own_ref, above_ref, below_ref, at + n, i) for n in (1, 2))
                deal(out_ref, ((d - 1) * tall + i) * TALL, coherence(re, im, powers[-2], powers[-1]))
        power, re, im = (whole_sum(next_ref, next_above_ref, next_below_ref, n, i) for n in range(3))
        deal(out_ref, ((span - 1) * tall + i) * TALL, coherence(re, im, powers[-1], power))
        power_ref[i] = power


def last_finish_kernel(own_ref, above_ref, below_ref, power_ref, out_ref):
    for i in range(own_ref.shape[1]):
        power, re, im = (whole_sum(own_ref, above_ref, below_ref, n, i) for n in range(3))
        deal(out_ref, i * TALL, coherence(re, im, power_ref[i], power))


def settle_kernel(got_ref, out_ref):
    group = got_ref.shape[0]
    pairs, tall = out_ref.shape[0], out_ref.shape[1] // (TALL * group)
    for device in range(group):
        strip = strip_of(device, group)
        for k in range(pairs):
            for i in range(tall):
                for r in range(TALL):
                    at = (k * tall + i) * TALL + r
                    row = (r * group + strip) * tall + i
                    out_ref[k, row : row + 1] = got_ref[device, at : at + 1]


def local(radar_subimages, owning_sector, sector_down_start, sector_across_start):
    group = lax.axis_size("grid")
    held, dates, planes, side, _ = radar_subimages.shape
    rows = side // group
    lines = group * TALL
    cols = WIDE * side
    span = dates - 2
    me = lax.axis_index("grid").astype(jnp.int32)
    devices = jnp.arange(group, dtype=jnp.int32)
    at = device_at(group)
    cells = radar_subimages.reshape(held, dates, planes, group, rows, side)
    cells = pltpu.with_memory_space_constraint(cells, pltpu.HBM)

    words = [
        pltpu.with_memory_space_constraint(word.reshape(1, held), pltpu.HBM)
        for word in (owning_sector, sector_down_start, sector_across_start)
    ]
    bulk = bulk_cut(*words, cells, span)
    got = lax.all_to_all(bulk, "grid", split_axis=0, concat_axis=0, tiled=True)
    strips = strip_of(shifted(me, devices, group), group)

    def scatter(date):
        sends = cut(strips, cells, date)
        pieces = [pltpu.with_memory_space_constraint(sends[0], pltpu.HBM)] + [None] * (group - 1)
        for m in range(1, group):
            pieces[m] = lax.ppermute(sends[m], "grid", [(i, shifted(i, m, group)) for i in range(group)])
        return pieces

    pieces_b = scatter(dates - 2)
    pieces = scatter(dates - 1)

    col = jnp.arange(cols)[:, None]
    out_col = jnp.arange(cols // 4)[None, :]
    window = ((col >= 4 * out_col - 12) & (col <= 4 * out_col + 15)).astype(jnp.bfloat16)
    window = pltpu.with_memory_space_constraint(window, pltpu.HBM)
    tags = got[:, -1, :2, :held].astype(jnp.int32)
    places = tags[:, 1] * lines + tags[:, 0]
    flat = places.reshape(group * held)
    counts = jnp.sum((flat[:, None] == flat[None, :]).astype(jnp.int32), axis=1)
    shares = 1.0 / jnp.maximum(counts, 1).astype(jnp.float32)
    tables = (flat, shares)
    swapped = tuple(t.reshape(group, held)[shifted(me, devices, group, -1)].reshape(group * held) for t in tables)
    tables, swapped = lax.optimization_barrier((tables, swapped))

    def exchange(up, down):
        below = lax.ppermute(up, "grid", [(at[s], at[s - 1]) for s in range(group)])
        above = lax.ppermute(down, "grid", [(at[s - 1], at[s]) for s in range(group)])
        return above, below

    window_bufs = [pltpu.VMEM(window.shape, window.dtype), pltpu.SemaphoreType.DMA(())]

    def piece_bufs(many):
        return [pltpu.VMEM((many, *pieces[0].shape), pieces[0].dtype), pltpu.SemaphoreType.DMA((many,))]

    comp = pltpu.VMEM((lines * WIDE, planes, rows, side), jnp.float32)
    out_cols = cols // 4
    tall = rows // 4
    outs, sums = sums_of(3 * span - 2, rows, lines, out_cols)
    kept, own, up, down = call(
        functools.partial(bulk_step_kernel, group=group, held=held),
        (strips, *tables), (got, window), [comp, *outs],
        [*window_bufs, pltpu.VMEM(got.shape, got.dtype), pltpu.SemaphoreType.DMA((group,)), sums] + [comp] * (span - 1),
        mib=16, remote=2,
    )
    above, below = exchange(up, down)
    outs, sums = sums_of(3, rows, lines, out_cols)
    kept, *next_sums = call(
        functools.partial(step_kernel, group=group, held=held),
        (strips, *swapped), (*pieces_b, window, kept), [comp, *outs],
        [*window_bufs, *piece_bufs(group), sums], remote=group + 1,
    )
    next_own, up, down = next_sums
    next_above, next_below = exchange(up, down)
    dealt, power = call(
        functools.partial(bulk_finish_kernel, span=span), (),
        (own, above, below, next_own, next_above, next_below),
        [
            jax.ShapeDtypeStruct((group, span * tall * TALL, out_cols), jnp.float32),
            jax.ShapeDtypeStruct((tall, lines, out_cols), jnp.float32),
        ],
    )

    ahead, level, late = started(group)
    near, middle, far = [0, *level, *ahead[: len(ahead) // 2]], ahead[len(ahead) // 2 :], late
    (part,) = call(
        functools.partial(part_kernel, names=near, held=held), swapped, [pieces[m] for m in near], [comp],
        piece_bufs(len(near)), remote=len(near),
    )
    (part,) = call(
        functools.partial(part_kernel, names=middle, held=held), swapped, (*[pieces[m] for m in middle], part), [comp],
        piece_bufs(len(middle)), aliases={2 + len(middle): 0}, remote=len(middle),
    )
    far_pieces = [pieces[m] for m in far]
    _, own, up, down = call(
        functools.partial(last_step_kernel, group=group, names=far, held=held),
        (strips, *swapped), (*far_pieces, window, kept, part), [comp, *outs],
        [*window_bufs, *piece_bufs(len(far)), sums], aliases={3 + len(far) + 2: 0},
        remote=len(far) + 1,
    )
    above, below = exchange(up, down)
    (last,) = call(
        last_finish_kernel, (), (own, above, below, power),
        [jax.ShapeDtypeStruct((group, tall * TALL, out_cols), jnp.float32)],
    )
    dealt = jnp.concatenate([dealt, last], axis=1)
    got = lax.all_to_all(dealt, "grid", split_axis=0, concat_axis=0, tiled=True)
    (out,) = call(
        settle_kernel, (), (got,),
        [jax.ShapeDtypeStruct((dates - 1, TALL * side // 4, out_cols), jnp.float32)],
    )
    return out


def solution(mesh):
    in_specs = (
        P(("region", "grid"), None, None, None, None),
        P(("region", "grid"), None),
        P(("region", "grid")),
        P(("region", "grid")),
    )
    out_specs = P(None, ("region", "grid"), None)

    return jax.shard_map(local, mesh=mesh, in_specs=in_specs, out_specs=out_specs, check_vma=False)
```

```python
import functools

import jax
import jax.numpy as jnp
from jax import lax
from jax.experimental import pallas as pl
from jax.experimental.pallas import tpu as pltpu
from jax.sharding import PartitionSpec as P


TALL = 4
WIDE = 8
EPSILON = 1e-06
LANES = 128
VMEM = pl.BlockSpec(memory_space=pltpu.VMEM)
HBM = pl.BlockSpec(memory_space=pltpu.HBM)


def strip_of(device, group):
    if group % 4:
        return device
    column, side, core = device // 4, (device // 2) % 2, device % 2
    return side * (group // 2) + 2 * (column + side * (group // 4 - 1 - 2 * column)) + core


def shifted(device, m, group, sign=1):
    if group % 4:
        return (device + sign * m) % group
    return ((device // 4 + sign * (m // 4)) % (group // 4)) * 4 + ((device % 4) ^ (m % 4))


def started(group):
    steps = group // 4 if group % 4 == 0 else group
    width = group // steps
    half = steps // 2
    order = [c for n in range(1, half) for c in (steps - n, n)]
    order += [c for c in range(1, steps) if c not in order]
    ahead = [m for c in order[:-1] for m in range(c * width, (c + 1) * width)]
    return ahead, list(range(1, width)), list(range(order[-1] * width, (order[-1] + 1) * width))


def device_at(group):
    places = [strip_of(d, group) for d in range(group)]
    return [places.index(s) for s in range(group)]


def bulk_kernel(*refs, span):
    words, (cells_ref, out_ref, *bufs, in_buf, out_buf, tag_buf, word_sem, in_sem, out_sem) = refs[:3], refs[3:]
    parts, each = in_buf.shape[:2]
    group, _, rows, side = out_buf.shape
    planes = in_buf.shape[3]
    held = parts * each
    many = each * span * planes
    fetches = [
        pltpu.make_async_copy(cells_ref.at[pl.ds(j * each, each), pl.ds(0, span)], in_buf.at[j], in_sem.at[j])
        for j in range(parts)
    ]
    small = [pltpu.make_async_copy(word, buf, word_sem.at[n]) for n, (word, buf) in enumerate(zip(words, bufs))]
    for fetch in small + fetches:
        fetch.start()
    stores = []
    for j, fetch in enumerate(fetches):
        fetch.wait()
        more = j == parts - 1
        if more:
            for copy in small:
                copy.wait()
            owner_ref, down_ref, across_ref = bufs
            tag_buf[...] = jnp.zeros(tag_buf.shape, jnp.float32)
            tag_buf[0:1, :held] = (owner_ref[...] * TALL + down_ref[...]).astype(jnp.float32)
            tag_buf[1:2, :held] = across_ref[...].astype(jnp.float32)
            tag = tag_buf[...].astype(out_buf.dtype)
        for g in range(group):
            strip = strip_of(g, group)
            out_buf[g, j * many : (j + 1) * many] = in_buf[j, :, :, :, strip].reshape(many, rows, side)
            if more:
                out_buf[g, held * span * planes] = tag
            piece = pl.ds(j * many, many + more)
            stores.append(pltpu.make_async_copy(out_buf.at[g, piece], out_ref.at[g, piece], out_sem.at[j, g]))
            stores[-1].start()
    for store in stores:
        store.wait()


def bulk_cut(owner, down, across, cells, span):
    held, _, planes, group, rows, side = cells.shape
    parts = next(p for p in (6, 4, 3, 2, 1) if held % p == 0)
    out = jax.ShapeDtypeStruct((group, held * span * planes + 1, rows, side), cells.dtype)
    return pl.pallas_call(
        functools.partial(bulk_kernel, span=span),
        out_shape=pltpu.HBM(out.shape, out.dtype),
        in_specs=[HBM] * 4,
        out_specs=HBM,
        scratch_shapes=[
            *[pltpu.VMEM((1, held), jnp.int32)] * 3,
            pltpu.VMEM((parts, held // parts, span, planes, group, rows, side), cells.dtype),
            pltpu.VMEM(out.shape, out.dtype),
            pltpu.VMEM((rows, side), jnp.float32),
            pltpu.SemaphoreType.DMA((3,)),
            pltpu.SemaphoreType.DMA((parts,)),
            pltpu.SemaphoreType.DMA((parts, group)),
        ],
        compiler_params=pltpu.CompilerParams(vmem_limit_bytes=12 << 20),
        name="bulk_cut",
    )(owner, down, across, cells)


def cut_kernel(strip_ref, cells_ref, *outs):
    held, _, planes, _, rows, side = cells_ref.shape
    for m, out in enumerate(outs):
        out[...] = cells_ref[:, 0, :, strip_ref[m]].reshape(held * planes, rows, side)


def cut(strips, cells, date):
    held, _, planes, group, rows, side = cells.shape
    piece = (held * planes, rows, side)
    return pl.pallas_call(
        cut_kernel,
        out_shape=[pltpu.HBM(piece, cells.dtype)] * group,
        grid_spec=pltpu.PrefetchScalarGridSpec(
            num_scalar_prefetch=1,
            grid=(1,),
            in_specs=[pl.BlockSpec((held, 1, planes, group, rows, side), lambda i, strips: (0, date, 0, 0, 0, 0))],
            out_specs=[pl.BlockSpec(piece, lambda i, strips: (0, 0, 0))] * group,
        ),
        compiler_params=pltpu.CompilerParams(vmem_limit_bytes=10 << 20),
        name="cut",
    )(strips, cells)


def gather(place_ref, share_ref, pieces, fetches, comps, names, held):
    span, planes = len(comps), comps[0].shape[1]
    for name, piece, fetch in zip(names, pieces, fetches):
        fetch.wait()

        def add(k, carry, name=name, piece=piece):
            place = place_ref[name * held + k]
            share = share_ref[name * held + k]
            for d, comp in enumerate(comps):
                for q in range(planes):
                    comp[place, q] += piece[(k * span + d) * planes + q].astype(jnp.float32) * share
            return carry

        lax.fori_loop(0, held, add, 0, unroll=4)


def start_all(sources, buf_ref, sems):
    fetches = [pltpu.make_async_copy(source, buf_ref.at[m], sems.at[m]) for m, source in enumerate(sources)]
    for fetch in fetches:
        fetch.start()
    return [buf_ref.at[m] for m in range(len(sources))], fetches


def box_sums(strip, comps, window_ref, window_copy, sums_ref, own_ref, up_ref, down_ref, group, skip):
    slots, _, rows, side = comps[0].shape
    lines = slots // WIDE
    step = min(lines, 16)
    window_copy.wait()
    window = window_ref[...]

    def row_of(comp, q, at):
        parts = [comp[pl.ds(c * lines + at, step), q].reshape(step * rows, side) for c in range(WIDE)]
        return jnp.concatenate(parts, axis=1)

    def emit(index, field, at):
        high = field.astype(jnp.bfloat16)
        low = (field - high.astype(jnp.float32)).astype(jnp.bfloat16)
        total = jnp.dot(high, window, preferred_element_type=jnp.float32)
        total += jnp.dot(low, window, preferred_element_type=jnp.float32)
        for half in range(sums_ref.shape[1]):
            sums_ref[index, half, pl.ds(at * rows, step * rows), :] = total[:, half * LANES : (half + 1) * LANES]

    for number in range(lines // step):
        at = number * step
        index = 0
        re_old = im_old = None
        for d, comp in enumerate(comps):
            re, im = row_of(comp, 0, at), row_of(comp, 1, at)
            if d >= skip:
                emit(index, re * re + im * im, at)
                index += 1
            if d:
                emit(index, re_old * re + im_old * im, at)
                emit(index + 1, im_old * re - re_old * im, at)
                index += 2
            re_old, im_old = re, im
    for f in range(sums_ref.shape[0]):
        level = [
            jnp.concatenate(
                [sums_ref[f, half, pl.ds(y, lines, stride=rows), :] for half in range(sums_ref.shape[1])], axis=1
            )
            for y in range(rows)
        ]
        for i in range(rows // 4):
            begin, end = max(0, 4 * i - 1), min(rows, 4 * i + 6)
            own_ref[f, i] = sum(level[begin + 1 : end], level[begin])
        up, down = level[0] + level[1], level[rows - 1]
        line = lax.broadcasted_iota(jnp.int32, up.shape, 0)
        up_next = jnp.where(line == lines - 1, 0.0, pltpu.roll(up, lines - 1, 0))
        down_next = jnp.where(line == 0, 0.0, pltpu.roll(down, 1, 0))
        up_ref[f] = jnp.where(strip == 0, up_next, up)
        down_ref[f] = jnp.where(strip == group - 1, down_next, down)


def begin(window_hbm, window_ref, window_sem, sources, buf_ref, sems, comps):
    views, fetches = start_all(sources, buf_ref, sems)
    window_copy = pltpu.make_async_copy(window_hbm, window_ref, window_sem)
    window_copy.start()
    for comp in comps:
        comp[...] = jnp.zeros(comp.shape, jnp.float32)
    return views, fetches, window_copy


def bulk_step_kernel(strip_ref, place_ref, share_ref, got_ref, window_hbm, kept_ref, own_ref, up_ref, down_ref, *scratch, group, held):
    window_ref, window_sem, buf_ref, sems, sums_ref, *fresh = scratch
    comps = [*fresh, kept_ref]
    sources = [got_ref.at[m] for m in range(group)]
    views, fetches, window_copy = begin(window_hbm, window_ref, window_sem, sources, buf_ref, sems, comps)
    gather(place_ref, share_ref, views, fetches, comps, range(group), held)
    box_sums(strip_ref[0], comps, window_ref, window_copy, sums_ref, own_ref, up_ref, down_ref, group, 0)


def step_kernel(strip_ref, place_ref, share_ref, *refs, group, held):
    pieces, (window_hbm, before_ref, comp, own_ref, up_ref, down_ref) = refs[:group], refs[group : group + 6]
    window_ref, window_sem, buf_ref, sems, sums_ref = refs[group + 6 :]
    views, fetches, window_copy = begin(window_hbm, window_ref, window_sem, pieces, buf_ref, sems, [comp])
    gather(place_ref, share_ref, views, fetches, [comp], range(group), held)
    box_sums(strip_ref[0], [before_ref, comp], window_ref, window_copy, sums_ref, own_ref, up_ref, down_ref, group, 1)


def part_kernel(place_ref, share_ref, *refs, names, held):
    pieces, (*old, comp, buf_ref, sems) = refs[: len(names)], refs[len(names) :]
    views, fetches = start_all(pieces, buf_ref, sems)
    if not old:
        comp[...] = jnp.zeros(comp.shape, jnp.float32)
    gather(place_ref, share_ref, views, fetches, [comp], names, held)


def last_step_kernel(strip_ref, place_ref, share_ref, *refs, group, names, held):
    many = len(names)
    pieces, (window_hbm, before_ref, _, comp, own_ref, up_ref, down_ref) = refs[:many], refs[many : many + 7]
    window_ref, window_sem, buf_ref, sems, sums_ref = refs[many + 7 :]
    views, fetches, window_copy = begin(window_hbm, window_ref, window_sem, pieces, buf_ref, sems, [])
    gather(place_ref, share_ref, views, fetches, [comp], names, held)
    box_sums(strip_ref[0], [before_ref, comp], window_ref, window_copy, sums_ref, own_ref, up_ref, down_ref, group, 1)


def sums_of(fields, rows, lines, cols):
    outs = [(fields, rows // 4, lines, cols), (fields, lines, cols), (fields, lines, cols)]
    return [jax.ShapeDtypeStruct(s, jnp.float32) for s in outs], pltpu.VMEM((fields, cols // LANES, lines * rows, LANES), jnp.float32)


def call(kernel, prefetch, args, outs, scratch=(), aliases=None, mib=12, remote=0):
    return pl.pallas_call(
        kernel,
        out_shape=outs,
        grid_spec=pltpu.PrefetchScalarGridSpec(
            num_scalar_prefetch=len(prefetch),
            grid=(),
            in_specs=[HBM] * remote + [VMEM] * (len(args) - remote),
            out_specs=[VMEM] * len(outs),
            scratch_shapes=list(scratch),
        ),
        input_output_aliases=aliases or {},
        compiler_params=pltpu.CompilerParams(vmem_limit_bytes=mib << 20),
    )(*prefetch, *args)


def whole_sum(own_ref, above_ref, below_ref, f, i):
    total = own_ref[f, i]
    if i == 0:
        total = total + above_ref[f]
    if i == own_ref.shape[1] - 1:
        total = total + below_ref[f]
    return total


def coherence(re, im, first, second):
    return jnp.sqrt(re * re + im * im) / jnp.sqrt(first * second + EPSILON)


def deal(out_ref, at, value):
    for g in range(out_ref.shape[0]):
        out_ref[g, at : at + TALL] = value[g * TALL : (g + 1) * TALL]


def bulk_finish_kernel(own_ref, above_ref, below_ref, next_ref, next_above_ref, next_below_ref, out_ref, power_ref, *, span):
    tall = own_ref.shape[1]
    for i in range(tall):
        powers = []
        for d in range(span):
            at = 0 if d == 0 else 3 * d - 2
            powers.append(whole_sum(own_ref, above_ref, below_ref, at, i))
            if d:
                re, im = (whole_sum(own_ref, above_ref, below_ref, at + n, i) for n in (1, 2))
                deal(out_ref, ((d - 1) * tall + i) * TALL, coherence(re, im, powers[-2], powers[-1]))
        power, re, im = (whole_sum(next_ref, next_above_ref, next_below_ref, n, i) for n in range(3))
        deal(out_ref, ((span - 1) * tall + i) * TALL, coherence(re, im, powers[-1], power))
        power_ref[i] = power


def last_finish_kernel(own_ref, above_ref, below_ref, power_ref, out_ref):
    for i in range(own_ref.shape[1]):
        power, re, im = (whole_sum(own_ref, above_ref, below_ref, n, i) for n in range(3))
        deal(out_ref, i * TALL, coherence(re, im, power_ref[i], power))


def settle_kernel(got_ref, out_ref):
    group = got_ref.shape[0]
    pairs, tall = out_ref.shape[0], out_ref.shape[1] // (TALL * group)
    for device in range(group):
        strip = strip_of(device, group)
        for k in range(pairs):
            for i in range(tall):
                for r in range(TALL):
                    at = (k * tall + i) * TALL + r
                    row = (r * group + strip) * tall + i
                    out_ref[k, row : row + 1] = got_ref[device, at : at + 1]


def local(radar_subimages, owning_sector, sector_down_start, sector_across_start):
    group = lax.axis_size("grid")
    held, dates, planes, side, _ = radar_subimages.shape
    rows = side // group
    lines = group * TALL
    cols = WIDE * side
    span = dates - 2
    me = lax.axis_index("grid").astype(jnp.int32)
    devices = jnp.arange(group, dtype=jnp.int32)
    at = device_at(group)
    cells = radar_subimages.reshape(held, dates, planes, group, rows, side)
    cells = pltpu.with_memory_space_constraint(cells, pltpu.HBM)

    words = [
        pltpu.with_memory_space_constraint(word.reshape(1, held), pltpu.HBM)
        for word in (owning_sector, sector_down_start, sector_across_start)
    ]
    bulk = bulk_cut(*words, cells, span)
    got = lax.all_to_all(bulk, "grid", split_axis=0, concat_axis=0, tiled=True)
    strips = strip_of(shifted(me, devices, group), group)

    def scatter(date):
        sends = cut(strips, cells, date)
        pieces = [pltpu.with_memory_space_constraint(sends[0], pltpu.HBM)] + [None] * (group - 1)
        for m in range(1, group):
            pieces[m] = lax.ppermute(sends[m], "grid", [(i, shifted(i, m, group)) for i in range(group)])
        return pieces

    pieces_b = scatter(dates - 2)
    pieces = scatter(dates - 1)

    col = jnp.arange(cols)[:, None]
    out_col = jnp.arange(cols // 4)[None, :]
    window = ((col >= 4 * out_col - 12) & (col <= 4 * out_col + 15)).astype(jnp.bfloat16)
    window = pltpu.with_memory_space_constraint(window, pltpu.HBM)
    tags = got[:, -1, :2, :held].astype(jnp.int32)
    places = tags[:, 1] * lines + tags[:, 0]
    flat = places.reshape(group * held)
    counts = jnp.sum((flat[:, None] == flat[None, :]).astype(jnp.int32), axis=1)
    shares = 1.0 / jnp.maximum(counts, 1).astype(jnp.float32)
    tables = (flat, shares)
    swapped = tuple(t.reshape(group, held)[shifted(me, devices, group, -1)].reshape(group * held) for t in tables)
    tables, swapped = lax.optimization_barrier((tables, swapped))

    def exchange(up, down):
        below = lax.ppermute(up, "grid", [(at[s], at[s - 1]) for s in range(group)])
        above = lax.ppermute(down, "grid", [(at[s - 1], at[s]) for s in range(group)])
        return above, below

    window_bufs = [pltpu.VMEM(window.shape, window.dtype), pltpu.SemaphoreType.DMA(())]

    def piece_bufs(many):
        return [pltpu.VMEM((many, *pieces[0].shape), pieces[0].dtype), pltpu.SemaphoreType.DMA((many,))]

    comp = pltpu.VMEM((lines * WIDE, planes, rows, side), jnp.float32)
    out_cols = cols // 4
    tall = rows // 4
    outs, sums = sums_of(3 * span - 2, rows, lines, out_cols)
    kept, own, up, down = call(
        functools.partial(bulk_step_kernel, group=group, held=held),
        (strips, *tables), (got, window), [comp, *outs],
        [*window_bufs, pltpu.VMEM(got.shape, got.dtype), pltpu.SemaphoreType.DMA((group,)), sums] + [comp] * (span - 1),
        mib=16, remote=2,
    )
    above, below = exchange(up, down)
    outs, sums = sums_of(3, rows, lines, out_cols)
    kept, *next_sums = call(
        functools.partial(step_kernel, group=group, held=held),
        (strips, *swapped), (*pieces_b, window, kept), [comp, *outs],
        [*window_bufs, *piece_bufs(group), sums], remote=group + 1,
    )
    next_own, up, down = next_sums
    next_above, next_below = exchange(up, down)
    dealt, power = call(
        functools.partial(bulk_finish_kernel, span=span), (),
        (own, above, below, next_own, next_above, next_below),
        [
            jax.ShapeDtypeStruct((group, span * tall * TALL, out_cols), jnp.float32),
            jax.ShapeDtypeStruct((tall, lines, out_cols), jnp.float32),
        ],
    )

    ahead, level, late = started(group)
    near, middle, far = [0, *level, *ahead[: len(ahead) // 2]], ahead[len(ahead) // 2 :], late
    (part,) = call(
        functools.partial(part_kernel, names=near, held=held), swapped, [pieces[m] for m in near], [comp],
        piece_bufs(len(near)), remote=len(near),
    )
    (part,) = call(
        functools.partial(part_kernel, names=middle, held=held), swapped, (*[pieces[m] for m in middle], part), [comp],
        piece_bufs(len(middle)), aliases={2 + len(middle): 0}, remote=len(middle),
    )
    middle, far = far[: len(far) // 2], far[len(far) // 2 :]
    (part,) = call(
        functools.partial(part_kernel, names=middle, held=held), swapped, (*[pieces[m] for m in middle], part), [comp],
        piece_bufs(len(middle)), aliases={2 + len(middle): 0}, remote=len(middle),
    )
    far_pieces = [pieces[m] for m in far]
    _, own, up, down = call(
        functools.partial(last_step_kernel, group=group, names=far, held=held),
        (strips, *swapped), (*far_pieces, window, kept, part), [comp, *outs],
        [*window_bufs, *piece_bufs(len(far)), sums], aliases={3 + len(far) + 2: 0},
        remote=len(far) + 1,
    )
    above, below = exchange(up, down)
    (last,) = call(
        last_finish_kernel, (), (own, above, below, power),
        [jax.ShapeDtypeStruct((group, tall * TALL, out_cols), jnp.float32)],
    )
    dealt = jnp.concatenate([dealt, last], axis=1)
    got = lax.all_to_all(dealt, "grid", split_axis=0, concat_axis=0, tiled=True)
    (out,) = call(
        settle_kernel, (), (got,),
        [jax.ShapeDtypeStruct((dates - 1, TALL * side // 4, out_cols), jnp.float32)],
    )
    return out


def solution(mesh):
    in_specs = (
        P(("region", "grid"), None, None, None, None),
        P(("region", "grid"), None),
        P(("region", "grid")),
        P(("region", "grid")),
    )
    out_specs = P(None, ("region", "grid"), None)

    return jax.shard_map(local, mesh=mesh, in_specs=in_specs, out_specs=out_specs, check_vma=False)
```
